256 devices in a mesh: site: 16 (over z_lo, x), phonon: 16 (over y, z_hi, core).
Axes of the slice: x: 4, y: 4, z: 8 (z_hi: 2, z_lo: 4; z = z_hi * 4 + z_lo), core: 2. Of those that a mesh axis runs over, the one named last changes fastest.
Arguments:
- state: float32 [16384, 2048], P('site', 'phonon'), may hold values from -4.5 to 6.5
- operators: bfloat16 [4, 1024, 1024], replicated, may hold values from -0.1875 to 0.1875
- op_mask: int32 [4, 8, 8], replicated, may hold values 0 or 1
- site_bits: int32 [4], replicated, may hold values from 0 to 3, each once
- field: float32 [4], replicated, may hold values from 0.25 to 1
- site_coupling: float32 [14], replicated, may hold values from 0.1 to 0.6
- mode_coupling: float32 [64], replicated, may hold values from 0.2 to 1
Outputs:
- chebyshev_last: float32 [16384, 2048], P('site', 'phonon')
- chebyshev_prev: float32 [16384, 2048], P('site', 'phonon')
- moments: float32 [3], replicated
The draws below stay inside these ranges and needn't reach their ends.
Inputs may be any that keep to these rules, and one draw needn't show every extreme that they name: `site_bits`: each of 0 to 3 exactly once.
All inputs are finite; a program needn't handle non-finite values.
Results may differ from the reference program's by a relative error of at most 0.0011.
The reference program's roundings to bfloat16 on the way (of `masked`) count: a program that leaves them out, or rounds other values in their place, can miss the bound.
Values sent between devices are 32-bit elements; how exact they have to be, the bound alone decides.
A program may use at most 64 MiB of HBM per device.

```python
import math
import jax
import jax.numpy as jnp

LBITS = 10
SBITS = 4
SITES = 14
CS = 1024
BLOCK = 128
NB = 8
MODES = 64
STEPS = 3
NLEV = 32
NS = 16384
NP = 2048
N_SITE = 16


def draw_state(key, part):
    row_place = jnp.arange(NS, dtype=jnp.float32)[:, None]
    column_place = jnp.arange(NP, dtype=jnp.float32)[None, :]
    smooth_part = 1.0 + 0.5 * jnp.cos(2.0 * math.pi * row_place / NS) * jnp.cos(math.pi * column_place / NP)
    noisy_part = jnp.clip(jax.random.normal(key, (NS, NP), jnp.float32), -5.0, 5.0)
    return (smooth_part + noisy_part).astype(jnp.float32)


def set_ends(values, rng, least, largest):
    dims = values.shape
    spot = [jax.random.randint(jax.random.fold_in(rng, axis), (), 0, dims[axis]) for axis in range(len(dims))]
    values = values.at[tuple(spot)].set(least)
    longest = dims.index(max(dims))
    spot[longest] = (spot[longest] + 1) % dims[longest]
    return values.at[tuple(spot)].set(largest)


def normal_values(key, extent, deviation, reach, held_as=jnp.bfloat16):
    values = jax.random.normal(key, extent, jnp.float32) * deviation
    return jnp.minimum(jnp.maximum(values, -reach), reach).astype(held_as)


def setup_inputs(seed: int = 0) -> dict:
    key_of = jax.random.split(jax.random.key(seed), 8)
    state = draw_state(jax.random.fold_in(key_of[7], 71), 0)
    operators = normal_values(key_of[1], (SBITS, CS, CS), CS ** -0.5, 0.1875)
    op_mask = set_ends((jax.random.randint(key_of[2], (SBITS, NB, NB), 0, 2) < 1).astype(jnp.int32), jax.random.fold_in(key_of[2], 1), 0, 1)
    site_bits = jax.random.permutation(key_of[3], SBITS).astype(jnp.int32)
    field = jnp.clip(jnp.exp(jax.random.uniform(key_of[4], (SBITS,), jnp.float32, math.log(0.25), math.log(1.0))), 0.25, 1.0)
    site_coupling = jnp.clip(jnp.exp(jax.random.uniform(key_of[5], (SITES,), jnp.float32, math.log(0.1), math.log(0.6))), 0.1, 0.6)
    mode_coupling = jnp.clip(jnp.exp(jax.random.uniform(key_of[6], (MODES,), jnp.float32, math.log(0.2), math.log(1.0))), 0.2, 1.0)
    return {"state": state, "operators": operators, "op_mask": op_mask, "site_bits": site_bits, "field": field, "site_coupling": site_coupling, "mode_coupling": mode_coupling}


epsilon = 1e-06

def flip_sites(values, position):
    shaped = values.reshape(N_SITE >> position + 1, 2, 1 << position, CS, NP)
    return shaped[:, ::-1].reshape(N_SITE, CS, NP)

def reference(state, operators, op_mask, site_bits, field, site_coupling, mode_coupling):
    expanded = jnp.repeat(jnp.repeat(op_mask, BLOCK, axis=1), BLOCK, axis=2)
    masked = jnp.where(expanded > 0, operators, jnp.zeros((), jnp.bfloat16))
    row_index = jnp.arange(NS, dtype=jnp.int32)
    device = row_index // CS
    inside = row_index % CS
    weight_rows = jnp.zeros((NS,), jnp.float32)
    for position in range(SBITS):
        weight_rows = weight_rows + site_coupling[site_bits[position]] * (device >> position & 1).astype(jnp.float32)
    for local_bit in range(LBITS):
        weight_rows = weight_rows + site_coupling[SBITS + local_bit] * (inside >> local_bit & 1).astype(jnp.float32)
    column = jnp.arange(NP, dtype=jnp.int32)
    levels = (column // MODES).astype(jnp.float32)
    lower_weight = jnp.sqrt(levels)
    upper_weight = jnp.sqrt(levels + 1.0)
    mode_weight = jnp.tile(mode_coupling, NP // MODES) / jnp.sqrt(jnp.float32(NLEV))
    entries = jnp.float32(NS * NP)

    def operate(vector):
        lower_part = jnp.pad(vector, ((0, 0), (MODES, 0)))[:, :NP]
        upper_part = jnp.pad(vector, ((0, 0), (0, MODES)))[:, MODES:]
        summed = weight_rows[:, None] * (mode_weight * (lower_weight * lower_part + upper_weight * upper_part))
        cube = vector.reshape(N_SITE, CS, NP)
        rounded = cube.astype(jnp.bfloat16).transpose(1, 0, 2).reshape(CS, N_SITE * NP)
        for position in range(SBITS):
            chosen = site_bits[position]
            product = jnp.dot(masked[chosen], rounded, preferred_element_type=jnp.float32)
            product = product.reshape(CS, N_SITE, NP).transpose(1, 0, 2)
            contribution = field[chosen] * cube + product
            summed = summed + flip_sites(contribution, position).reshape(NS, NP)
        return summed

    def root_mean(values):
        return jnp.sqrt(jnp.sum(values * values) / entries + epsilon)
    initial = state / root_mean(state)
    previous = initial
    current = initial
    scale_prev = jnp.float32(1.0)
    moments = []
    for iteration in range(STEPS):
        applied = operate(current)
        if iteration == 0:
            vector_new = applied
        else:
            vector_new = 2.0 * applied - previous / scale_prev
        scale_now = root_mean(vector_new)
        updated = vector_new / scale_now
        moments.append(jnp.sum(initial * updated) / entries)
        previous = current
        current = updated
        scale_prev = scale_now
    return (current, previous, jnp.stack(moments))
```

```python
import functools
import jax
import jax.numpy as jnp
from jax import lax
from jax.experimental import pallas as pl
from jax.experimental.pallas import tpu as pltpu
from jax.sharding import PartitionSpec as P

MESH = pl.DeviceIdType.MESH
F32 = jnp.float32
BF16 = jnp.bfloat16
ROWS = 1024
LANES = 128
STEPS = 3
EPSILON = 1e-06
ENTRIES = 33554432.0


def flipped(value, bit):
    size = 8 << bit
    parts = [value[i * size : (i + 1) * size] for i in range(LANES // size)]
    swapped = []
    for i in range(0, len(parts), 2):
        swapped += [parts[i + 1], parts[i]]
    return jnp.concatenate(swapped, axis=0)


def kernel(
    state, ops, mask, site_bits, field, site_coupling, mode_coupling,
    last, prev, moments,
    st, opv, a, t, r_in, r_2, r_3, w_1, w_2, w_3, u_0, u_1, u_2, ub, acc, occ, halo,
    sc_a, sc_b, ss_a, ss_b, out_2, out_3,
    load_sem, self_sem, out_sem, send_sem, recv_sem, hsend_sem, hrecv_sem,
    asend_sem, arecv_sem, bsend_sem, brecv_sem,
):
    site = lax.axis_index("site")
    phonon = lax.axis_index("phonon")
    z_lo, x = site // 4, site % 4
    y, q = phonon // 4, phonon % 4
    z_hi, core = q // 2, q % 2
    z = z_hi * 4 + z_lo
    mode = site * 4 + q
    index_a = x * 8 + y * 2 + core

    load_state = pltpu.make_async_copy(state, st, load_sem.at[0])
    load_state.start()
    load_ops = pltpu.make_async_copy(ops, opv, load_sem.at[1])
    load_ops.start()

    barrier = pltpu.get_barrier_semaphore()

    def plane(k):
        other = (mode + k) % 64
        return other, (other // 4, y * 4 + other % 4)

    def stage_a(k):
        other = (index_a + k) % 32
        return other, (z_lo * 4 + other // 8, ((other // 2) % 4) * 4 + z_hi * 2 + other % 2)

    def stage_b(k):
        other = (z + k) % 8
        return other, ((other % 4) * 4 + x, y * 4 + (other // 4) * 2 + core)

    @pl.loop(1, 64)
    def _(k):
        pl.semaphore_signal(barrier, inc=1, device_id=plane(k)[1], device_id_type=MESH)

    @pl.loop(0, 24)
    def _(k):
        y_other = (y + 1 + k // 8) % 4
        device = (z_lo * 4 + (k // 2) % 4, y_other * 4 + z_hi * 2 + k % 2)
        pl.semaphore_signal(barrier, inc=1, device_id=device, device_id_type=MESH)

    load_state.wait()
    zero = jnp.zeros((8, LANES), F32)
    squares = zero
    for high in range(8):
        block = st[high * 128 : (high + 1) * 128, :]
        squares = squares + jnp.sum((block * block).reshape(16, 8, LANES), axis=0)
        turned = block.T
        t[pl.ds(high, 64, stride=16), :] = turned[:64]
        t[pl.ds(8 + high, 64, stride=16), :] = turned[64:]

    lane = lax.broadcasted_iota(jnp.int32, (1, LANES), 1)

    def fold(value):
        row = jnp.sum(value, axis=0, keepdims=True)
        return row + pltpu.roll(row, 64, 1)

    def spread(src, dst_of, count, target, send, recv, index):
        @pl.loop(1, count)
        def _(k):
            other, device = target(k)
            pltpu.make_async_remote_copy(
                src_ref=src, dst_ref=dst_of(index), send_sem=send, recv_sem=recv,
                device_id=device, device_id_type=MESH,
            ).start()

    def scalars_start(r, squares, products):
        row = jnp.where(lane < 64, fold(squares), fold(products))
        ss_a[r] = row
        sc_a[r, index_a] = row
        spread(ss_a.at[r], lambda i: sc_a.at[r, i], 32, stage_a, asend_sem.at[r], arecv_sem.at[r], index_a)

    def wait_recv(ref, send, recv):
        pltpu.make_async_remote_copy(
            src_ref=ref, dst_ref=ref, send_sem=send, recv_sem=recv,
            device_id=(site, phonon), device_id_type=MESH,
        ).wait_recv()

    def wait_send(ref, send, recv):
        pltpu.make_async_remote_copy(
            src_ref=ref, dst_ref=ref, send_sem=send, recv_sem=recv,
            device_id=(site, phonon), device_id_type=MESH,
        ).wait_send()

    def scalars_middle(r):
        wait_recv(sc_a.at[r, pl.ds(0, 31)], asend_sem.at[r], arecv_sem.at[r])
        row = jnp.sum(sc_a[r], axis=0)
        ss_b[r] = row
        sc_b[r, z] = row
        spread(ss_b.at[r], lambda i: sc_b.at[r, i], 8, stage_b, bsend_sem.at[r], brecv_sem.at[r], z)

    def scalars_end(r):
        wait_recv(sc_b.at[r, pl.ds(0, 7)], bsend_sem.at[r], brecv_sem.at[r])
        row = jnp.sum(sc_b[r], axis=0)
        total = jnp.sum(jnp.where(lane < 64, row, 0.0), axis=1, keepdims=True)
        product = jnp.sum(jnp.where(lane < 64, 0.0, row), axis=1, keepdims=True)
        inverse = 1.0 / jnp.sqrt(total / ENTRIES + EPSILON)
        return inverse, product * inverse / ENTRIES

    def chunk2(ref, i):
        return ref.at[pl.ds(pl.multiple_of(i * 16, 16), 16), :]

    def chunk3(ref, i):
        return ref.at[i // 4, pl.ds(pl.multiple_of((i % 4) * 16, 16), 16), :]

    def exchange_start(e, src, src_chunk, dst, dst_chunk):
        pltpu.make_async_copy(src_chunk(src, mode), dst_chunk(dst, mode), self_sem.at[e]).start()

        @pl.loop(1, 64)
        def _(k):
            other, device = plane(k)
            pltpu.make_async_remote_copy(
                src_ref=src_chunk(src, other), dst_ref=dst_chunk(dst, mode),
                send_sem=send_sem.at[e], recv_sem=recv_sem.at[e],
                device_id=device, device_id_type=MESH,
            ).start()

    def exchange_wait(e, src, src_chunk, dst, dst_chunk):
        pltpu.make_async_copy(src_chunk(src, mode), dst_chunk(dst, mode), self_sem.at[e]).wait()
        wait_recv(t.at[pl.ds(0, 63 * 16), :], send_sem.at[e], recv_sem.at[e])

    def halo_copies(k, w):
        up = pltpu.make_async_remote_copy(
            src_ref=w.at[:, pl.ds(56, 8), :], dst_ref=halo.at[k, 0],
            send_sem=hsend_sem.at[k, 0], recv_sem=hrecv_sem.at[k, 0],
            device_id=(site, ((y + 1) % 4) * 4 + q), device_id_type=MESH,
        )
        down = pltpu.make_async_remote_copy(
            src_ref=w.at[:, pl.ds(0, 8), :], dst_ref=halo.at[k, 1],
            send_sem=hsend_sem.at[k, 1], recv_sem=hrecv_sem.at[k, 1],
            device_id=(site, ((y + 3) % 4) * 4 + q), device_id_type=MESH,
        )
        return up, down

    pl.semaphore_wait(barrier, 87)
    scalars_start(0, squares, zero)
    exchange_start(0, t, chunk2, r_in, chunk3)

    chosen = [site_bits[b] for b in range(4)]
    fields = [field[c] for c in chosen]
    device_coupling = [site_coupling[c] for c in chosen]

    place = lax.broadcasted_iota(jnp.int32, (8, ROWS), 1)
    weights = jnp.zeros((8, ROWS), F32)
    for j in range(10):
        weights = weights + site_coupling[4 + j] * ((place >> j) & 1).astype(F32)
    occ[...] = weights

    level = lax.broadcasted_iota(jnp.int32, (8, LANES), 0) + y * 8
    mode_weight = mode_coupling[mode] / jnp.sqrt(F32(32.0))
    lower_weight = mode_weight * jnp.sqrt(level.astype(F32))
    upper_weight = mode_weight * jnp.where(level < 31, jnp.sqrt((level + 1).astype(F32)), 0.0)

    load_ops.wait()

    def mask_operator(b):
        @pl.loop(0, 8)
        def _(i):
            rows = pl.ds(pl.multiple_of(i * 128, 128), 128)
            for j in range(8):
                keep = mask[chosen[b] * 64 + i * 8 + j] > 0
                tile = opv[chosen[b], rows, j * 128 : (j + 1) * 128]
                a[b, rows, j * 128 : (j + 1) * 128] = jnp.where(keep, tile, jnp.zeros_like(tile))

    for b in range(4):
        mask_operator(b)
    scalars_middle(0)
    exchange_wait(0, t, chunk2, r_in, chunk3)
    for copy in halo_copies(0, r_in):
        copy.start()
    inverse, _ = scalars_end(0)

    sublane = lax.broadcasted_iota(jnp.int32, (8, LANES), 0)

    def normalize(w, u, inverse):
        scale = jnp.broadcast_to(inverse, (8, LANES))

        @pl.loop(0, 8)
        def _(e):
            for high in range(8):
                cols = slice(high * 128, (high + 1) * 128)
                first = w[2 * e, pl.ds(high, 8, stride=8), :] * scale
                second = w[2 * e + 1, pl.ds(high, 8, stride=8), :] * scale
                both = jnp.concatenate([first, second], axis=0)
                rows = pl.ds(pl.multiple_of(e * 16, 16), 16)
                u[rows, cols] = both
                ub[rows, cols] = both.astype(BF16)

    def step(k, u, u_before, w, inverse):
        scale = jnp.broadcast_to(inverse, (8, LANES))

        @pl.loop(0, 4)
        def _(c):
            cols = pl.ds(pl.multiple_of(c * 256, 256), 256)
            here = u[:, cols]
            total = None
            for b in range(4):
                product = lax.dot_general(
                    ub[...], a[b, cols, :], (((1,), (1,)), ((), ())), preferred_element_type=F32
                )
                moved = flipped(product + fields[b] * here, b)
                total = moved if total is None else total + moved
            acc[:, cols] = total

        for copy in halo_copies(k, w):
            copy.wait_recv()

        def body(d, carry):
            squares, products = carry
            constant = F32(0.0)
            for b in range(4):
                constant = constant + device_coupling[b] * ((d >> b) & 1).astype(F32)
            rows = pl.ds(pl.multiple_of(d * 8, 8), 8)
            for high in range(8):
                cols = slice(high * 128, (high + 1) * 128)
                here = u[rows, cols]
                below = jnp.broadcast_to(halo[k, 0, d, high : high + 1, :], (8, LANES)) * scale
                above = jnp.broadcast_to(halo[k, 1, d, high : high + 1, :], (8, LANES)) * scale
                lower = jnp.where(sublane == 0, below, pltpu.roll(here, 1, 0))
                upper = jnp.where(sublane == 7, above, pltpu.roll(here, 7, 0))
                ladder = (occ[:, cols] + constant) * (lower_weight * lower + upper_weight * upper)
                new = acc[rows, cols] + ladder
                if k > 0:
                    new = 2.0 * new - u_before[rows, cols] * scale
                w[d, pl.ds(high, 8, stride=8), :] = new
                squares = squares + new * new
                products = products + u_0[rows, cols] * new
            return squares, products

        return lax.fori_loop(0, 16, body, (zero, zero))

    def finish(r, inverse, out):
        scale = jnp.broadcast_to(inverse, (128, LANES))
        for high in range(8):
            block = jnp.concatenate(
                [r[pl.ds(high, 64, stride=16), :], r[pl.ds(8 + high, 64, stride=16), :]], axis=0
            )
            out[high * 128 : (high + 1) * 128, :] = block.T * scale

    def set_moment(k, value):
        moments[k] = value[0, 0]

    normalize(r_in, u_0, inverse)
    squares, products = step(0, u_0, u_0, w_1, inverse)
    scalars_start(1, squares, products)
    for copy in halo_copies(1, w_1):
        copy.start()
    scalars_middle(1)
    inverse, moment = scalars_end(1)
    set_moment(0, moment)

    normalize(w_1, u_1, inverse)
    squares, products = step(1, u_1, u_0, w_2, inverse)
    scalars_start(2, squares, products)
    for copy in halo_copies(2, w_2):
        copy.start()
    scalars_middle(2)
    inverse, moment = scalars_end(2)
    exchange_start(1, w_2, chunk3, r_2, chunk2)
    set_moment(1, moment)
    inverse_2 = inverse

    normalize(w_2, u_2, inverse)
    squares, products = step(2, u_2, u_1, w_3, inverse)
    scalars_start(3, squares, products)
    exchange_start(2, w_3, chunk3, r_3, chunk2)
    scalars_middle(3)
    exchange_wait(1, w_2, chunk3, r_2, chunk2)
    finish(r_2, inverse_2, out_2)
    store_2 = pltpu.make_async_copy(out_2, prev, out_sem.at[0])
    store_2.start()
    inverse, moment = scalars_end(3)
    set_moment(2, moment)
    exchange_wait(2, w_3, chunk3, r_3, chunk2)
    finish(r_3, inverse, out_3)
    store_3 = pltpu.make_async_copy(out_3, last, out_sem.at[1])
    store_3.start()

    for e in range(3):
        wait_send(t.at[pl.ds(0, 63 * 16), :], send_sem.at[e], recv_sem.at[e])
    for r in range(4):
        wait_send(sc_a.at[r, pl.ds(0, 31)], asend_sem.at[r], arecv_sem.at[r])
        wait_send(sc_b.at[r, pl.ds(0, 7)], bsend_sem.at[r], brecv_sem.at[r])
    for k, w in enumerate((r_in, w_1, w_2)):
        for copy in halo_copies(k, w):
            copy.wait_send()
    store_2.wait()
    store_3.wait()


def shards(state, operators, op_mask, site_bits, field, site_coupling, mode_coupling):
    block = jax.ShapeDtypeStruct((ROWS, LANES), F32)
    flat = pltpu.VMEM((ROWS, LANES), F32)
    cube = pltpu.VMEM((16, 64, LANES), F32)
    wide = pltpu.VMEM((LANES, ROWS), F32)
    dma = pltpu.SemaphoreType.DMA
    anywhere = pl.BlockSpec(memory_space=pl.ANY)
    scalar = pl.BlockSpec(memory_space=pltpu.SMEM)
    return pl.pallas_call(
        kernel,
        out_shape=(block, block, jax.ShapeDtypeStruct((STEPS,), F32)),
        in_specs=[anywhere, anywhere, scalar, scalar, scalar, scalar, scalar],
        out_specs=(anywhere, anywhere, scalar),
        scratch_shapes=[
            flat,
            pltpu.VMEM((4, ROWS, ROWS), BF16),
            pltpu.VMEM((4, ROWS, ROWS), BF16),
            flat,
            cube,
            flat,
            flat,
            cube,
            cube,
            cube,
            wide,
            wide,
            wide,
            pltpu.VMEM((LANES, ROWS), BF16),
            wide,
            pltpu.VMEM((8, ROWS), F32),
            pltpu.VMEM((3, 2, 16, 8, LANES), F32),
            pltpu.VMEM((4, 32, 1, LANES), F32),
            pltpu.VMEM((4, 8, 1, LANES), F32),
            pltpu.VMEM((4, 1, LANES), F32),
            pltpu.VMEM((4, 1, LANES), F32),
            flat,
            flat,
            dma((2,)),
            dma((3,)),
            dma((2,)),
            dma((3,)),
            dma((3,)),
            dma((3, 2)),
            dma((3, 2)),
            dma((4,)),
            dma((4,)),
            dma((4,)),
            dma((4,)),
        ],
        compiler_params=pltpu.CompilerParams(
            collective_id=0, has_side_effects=True, vmem_limit_bytes=48 * 1024 * 1024
        ),
    )(state, operators, op_mask.reshape(-1), site_bits, field, site_coupling, mode_coupling)


def solution(mesh):
    in_specs = (P("site", "phonon"), P(), P(), P(), P(), P(), P())
    out_specs = (P("site", "phonon"), P("site", "phonon"), P())
    return jax.shard_map(shards, mesh=mesh, in_specs=in_specs, out_specs=out_specs, check_vma=False)
```

```python
import functools
import jax
import jax.numpy as jnp
from jax import lax
from jax.experimental import pallas as pl
from jax.experimental.pallas import tpu as pltpu
from jax.sharding import PartitionSpec as P

MESH = pl.DeviceIdType.MESH
F32 = jnp.float32
BF16 = jnp.bfloat16
ROWS = 1024
LANES = 128
STEPS = 3
EPSILON = 1e-06
ENTRIES = 33554432.0


def flipped(value, bit):
    size = 8 << bit
    parts = [value[i * size : (i + 1) * size] for i in range(LANES // size)]
    swapped = []
    for i in range(0, len(parts), 2):
        swapped += [parts[i + 1], parts[i]]
    return jnp.concatenate(swapped, axis=0)


def ring(offset, size):
    return min(offset % size, -offset % size)


def offsets(zs=1, xs=1, ys=1, cores=1):
    found = [
        (dz, dx, dy, dc)
        for dz in range(zs)
        for dx in range(xs)
        for dy in range(ys)
        for dc in range(cores)
        if (dz, dx, dy, dc) != (0, 0, 0, 0)
    ]
    return sorted(found, key=lambda o: -ring(o[0], 8) - ring(o[1], 4) - ring(o[2], 4))


PLANE = offsets(zs=8, xs=4, cores=2)
LINE = offsets(ys=4)
COLUMN = offsets(zs=8, cores=2)
LAYER = offsets(xs=4, ys=4)


def kernel(
    state, ops, mask_in, site_bits_in, field_in, site_coupling_in, mode_coupling_in,
    last, prev, moments,
    mask, site_bits, field, site_coupling, mode_coupling,
    st, opv, a, t, r_in, r_2, r_3, w_1, w_2, w_3, u_0, u_1, u_2, ub, acc, occ, halo,
    slots_1, slots_2, rows_1, rows_2, out_2, out_3,
    load_sem, self_sem, out_sem, send_sem, recv_sem, hsend_sem, hrecv_sem,
    send_1, recv_1, send_2, recv_2,
):
    site = lax.axis_index("site")
    phonon = lax.axis_index("phonon")
    z_lo, x = site // 4, site % 4
    y, q = phonon // 4, phonon % 4
    z_hi, core = q // 2, q % 2
    z = z_hi * 4 + z_lo
    mode = site * 4 + q

    def place_of(offset):
        dz, dx, dy, dc = offset
        z_at, x_at, y_at, core_at = (z + dz) % 8, (x + dx) % 4, (y + dy) % 4, (core + dc) % 2
        return (z_at % 4) * 4 + x_at, y_at, (z_at // 4) * 2 + core_at

    def device_of(offset):
        site_at, y_at, q_at = place_of(offset)
        return (site_at, y_at * 4 + q_at)

    barrier = pltpu.get_barrier_semaphore()
    for offset in PLANE + LINE:
        pl.semaphore_signal(barrier, inc=1, device_id=device_of(offset), device_id_type=MESH)

    load_state = pltpu.make_async_copy(state, st, load_sem.at[0])
    load_state.start()
    load_ops = pltpu.make_async_copy(ops, opv, load_sem.at[1])
    small = [
        pltpu.make_async_copy(source, target, load_sem.at[2 + i])
        for i, (source, target) in enumerate(
            (
                (mask_in, mask),
                (site_bits_in, site_bits),
                (field_in, field),
                (site_coupling_in, site_coupling),
                (mode_coupling_in, mode_coupling),
            )
        )
    ]
    for copy in small:
        copy.start()
    load_ops.start()

    load_state.wait()
    zero = jnp.zeros((8, LANES), F32)
    squares = zero
    for high in range(8):
        block = st[high * 128 : (high + 1) * 128, :]
        squares = squares + jnp.sum((block * block).reshape(16, 8, LANES), axis=0)
        turned = block.T
        t[pl.ds(high, 64, stride=16), :] = turned[:64]
        t[pl.ds(8 + high, 64, stride=16), :] = turned[64:]

    lane = lax.broadcasted_iota(jnp.int32, (1, LANES), 1)

    def fold(value):
        row = jnp.sum(value, axis=0, keepdims=True)
        return row + pltpu.roll(row, 64, 1)

    def wait_recv(ref, send, recv):
        pltpu.make_async_remote_copy(
            src_ref=ref, dst_ref=ref, send_sem=send, recv_sem=recv,
            device_id=(site, phonon), device_id_type=MESH,
        ).wait_recv()

    def wait_send(ref, send, recv):
        pltpu.make_async_remote_copy(
            src_ref=ref, dst_ref=ref, send_sem=send, recv_sem=recv,
            device_id=(site, phonon), device_id_type=MESH,
        ).wait_send()

    groups = {
        "plane": (PLANE, 64, site * 4 + q),
        "line": (LINE, 4, y),
        "column": (COLUMN, 16, z * 2 + core),
        "layer": (LAYER, 16, x * 4 + y),
    }

    def spread(group, src, slots, row, send, recv):
        members, count, index = groups[group]
        src[...] = row
        slots[index] = row
        for offset in members:
            pltpu.make_async_remote_copy(
                src_ref=src, dst_ref=slots.at[index], send_sem=send, recv_sem=recv,
                device_id=device_of(offset), device_id_type=MESH,
            ).start()

    def gather(group, slots, send, recv):
        members, count, index = groups[group]
        wait_recv(slots.at[pl.ds(0, count - 1)], send, recv)
        return jnp.sum(slots[0:count], axis=0)

    def scalars_start(r, group, squares, products):
        row = jnp.where(lane < 64, fold(squares), fold(products))
        spread(group, rows_1.at[r], slots_1.at[r], row, send_1.at[r], recv_1.at[r])

    def scalars_middle(r, group, group_2):
        row = gather(group, slots_1.at[r], send_1.at[r], recv_1.at[r])
        spread(group_2, rows_2.at[r], slots_2.at[r], row, send_2.at[r], recv_2.at[r])

    def scalars_end(r, group_2):
        row = gather(group_2, slots_2.at[r], send_2.at[r], recv_2.at[r])
        total = jnp.sum(jnp.where(lane < 64, row, 0.0), axis=1, keepdims=True)
        product = jnp.sum(jnp.where(lane < 64, 0.0, row), axis=1, keepdims=True)
        inverse = 1.0 / jnp.sqrt(total / ENTRIES + EPSILON)
        return inverse, product * inverse / ENTRIES

    def chunk2(ref, i):
        return ref.at[pl.ds(pl.multiple_of(i * 16, 16), 16), :]

    def chunk3(ref, site_at, q_at):
        return ref.at[site_at, pl.ds(pl.multiple_of(q_at * 16, 16), 16), :]

    def exchange_in_self():
        return pltpu.make_async_copy(chunk2(t, mode), chunk3(r_in, site, q), self_sem.at[0])

    def exchange_in_start():
        exchange_in_self().start()
        for offset in PLANE:
            site_at, y_at, q_at = place_of(offset)
            pltpu.make_async_remote_copy(
                src_ref=chunk2(t, site_at * 4 + q_at), dst_ref=chunk3(r_in, site, q),
                send_sem=send_sem.at[0], recv_sem=recv_sem.at[0],
                device_id=(site_at, y_at * 4 + q_at), device_id_type=MESH,
            ).start()

    def exchange_in_wait():
        exchange_in_self().wait()
        wait_recv(t.at[pl.ds(0, 63 * 16), :], send_sem.at[0], recv_sem.at[0])

    def exchange_out_self(e, w, r):
        return pltpu.make_async_copy(chunk3(w, site, q), chunk2(r, mode), self_sem.at[e])

    def exchange_out_start(e, w, r):
        exchange_out_self(e, w, r).start()
        for offset in PLANE:
            site_at, y_at, q_at = place_of(offset)
            pltpu.make_async_remote_copy(
                src_ref=chunk3(w, site_at, q_at), dst_ref=chunk2(r, mode),
                send_sem=send_sem.at[e], recv_sem=recv_sem.at[e],
                device_id=(site_at, y_at * 4 + q_at), device_id_type=MESH,
            ).start()

    def exchange_out_wait(e, w, r):
        exchange_out_self(e, w, r).wait()
        wait_recv(t.at[pl.ds(0, 63 * 16), :], send_sem.at[e], recv_sem.at[e])

    def halo_copies(k, w):
        up = pltpu.make_async_remote_copy(
            src_ref=w.at[:, pl.ds(56, 8), :], dst_ref=halo.at[k, 0],
            send_sem=hsend_sem.at[k, 0], recv_sem=hrecv_sem.at[k, 0],
            device_id=(site, ((y + 1) % 4) * 4 + q), device_id_type=MESH,
        )
        down = pltpu.make_async_remote_copy(
            src_ref=w.at[:, pl.ds(0, 8), :], dst_ref=halo.at[k, 1],
            send_sem=hsend_sem.at[k, 1], recv_sem=hrecv_sem.at[k, 1],
            device_id=(site, ((y + 3) % 4) * 4 + q), device_id_type=MESH,
        )
        return up, down

    pl.semaphore_wait(barrier, 66)
    scalars_start(0, "plane", squares, zero)
    exchange_in_start()

    for copy in small:
        copy.wait()
    chosen = [site_bits[b] for b in range(4)]
    fields = [field[c] for c in chosen]
    device_coupling = [site_coupling[c] for c in chosen]

    place = lax.broadcasted_iota(jnp.int32, (8, ROWS), 1)
    weights = jnp.zeros((8, ROWS), F32)
    for j in range(10):
        weights = weights + site_coupling[4 + j] * ((place >> j) & 1).astype(F32)
    occ[...] = weights

    level = lax.broadcasted_iota(jnp.int32, (8, LANES), 0) + y * 8
    mode_weight = mode_coupling[mode] / jnp.sqrt(F32(32.0))
    lower_weight = mode_weight * jnp.sqrt(level.astype(F32))
    upper_weight = mode_weight * jnp.where(level < 31, jnp.sqrt((level + 1).astype(F32)), 0.0)

    load_ops.wait()

    def mask_operator(b):
        @pl.loop(0, 8)
        def _(i):
            rows = pl.ds(pl.multiple_of(i * 128, 128), 128)
            for j in range(8):
                keep = mask[chosen[b], i, j] > 0
                tile = opv[chosen[b], rows, j * 128 : (j + 1) * 128]
                a[b, rows, j * 128 : (j + 1) * 128] = jnp.where(keep, tile, jnp.zeros_like(tile))

    for b in range(4):
        mask_operator(b)
    scalars_middle(0, "plane", "line")
    exchange_in_wait()
    for copy in halo_copies(0, r_in):
        copy.start()
    inverse, _ = scalars_end(0, "line")

    sublane = lax.broadcasted_iota(jnp.int32, (8, LANES), 0)

    def normalize(w, u, inverse):
        scale = jnp.broadcast_to(inverse, (8, LANES))

        @pl.loop(0, 8)
        def _(e):
            for high in range(8):
                cols = slice(high * 128, (high + 1) * 128)
                first = w[2 * e, pl.ds(high, 8, stride=8), :] * scale
                second = w[2 * e + 1, pl.ds(high, 8, stride=8), :] * scale
                both = jnp.concatenate([first, second], axis=0)
                rows = pl.ds(pl.multiple_of(e * 16, 16), 16)
                u[rows, cols] = both
                ub[rows, cols] = both.astype(BF16)

    def step(k, u, u_before, w, inverse, send=None):
        scale = jnp.broadcast_to(inverse, (8, LANES))

        @pl.loop(0, 4)
        def _(c):
            cols = pl.ds(pl.multiple_of(c * 256, 256), 256)
            here = u[:, cols]
            total = None
            for b in range(4):
                product = lax.dot_general(
                    ub[...], a[b, cols, :], (((1,), (1,)), ((), ())), preferred_element_type=F32
                )
                moved = flipped(product + fields[b] * here, b)
                total = moved if total is None else total + moved
            acc[:, cols] = total

        for copy in halo_copies(k, w):
            copy.wait_recv()

        def body(i, carry):
            squares, products = carry
            d = (site + 1 + i) % 16
            constant = F32(0.0)
            for b in range(4):
                constant = constant + device_coupling[b] * ((d >> b) & 1).astype(F32)
            rows = pl.ds(pl.multiple_of(d * 8, 8), 8)
            for high in range(8):
                cols = slice(high * 128, (high + 1) * 128)
                here = u[rows, cols]
                below = jnp.broadcast_to(halo[k, 0, d, high : high + 1, :], (8, LANES)) * scale
                above = jnp.broadcast_to(halo[k, 1, d, high : high + 1, :], (8, LANES)) * scale
                lower = jnp.where(sublane == 0, below, pltpu.roll(here, 1, 0))
                upper = jnp.where(sublane == 7, above, pltpu.roll(here, 7, 0))
                ladder = (occ[:, cols] + constant) * (lower_weight * lower + upper_weight * upper)
                new = acc[rows, cols] + ladder
                if k > 0:
                    new = 2.0 * new - u_before[rows, cols] * scale
                w[d, pl.ds(high, 8, stride=8), :] = new
                squares = squares + new * new
                products = products + u_0[rows, cols] * new
            if send is not None:
                send(i)
            return squares, products

        return lax.fori_loop(0, 16, body, (zero, zero))

    def finish(r, inverse, out):
        scale = jnp.broadcast_to(inverse, (128, LANES))
        for high in range(8):
            block = jnp.concatenate(
                [r[pl.ds(high, 64, stride=16), :], r[pl.ds(8 + high, 64, stride=16), :]], axis=0
            )
            out[high * 128 : (high + 1) * 128, :] = block.T * scale

    def set_moment(k, value):
        moments[k] = value[0, 0]

    normalize(r_in, u_0, inverse)
    squares, products = step(0, u_0, u_0, w_1, inverse)
    scalars_start(1, "column", squares, products)
    for copy in halo_copies(1, w_1):
        copy.start()
    scalars_middle(1, "column", "layer")
    inverse, moment = scalars_end(1, "layer")
    set_moment(0, moment)

    normalize(w_1, u_1, inverse)
    squares, products = step(1, u_1, u_0, w_2, inverse)
    scalars_start(2, "column", squares, products)
    for copy in halo_copies(2, w_2):
        copy.start()
    exchange_out_start(1, w_2, r_2)
    scalars_middle(2, "column", "layer")
    inverse, moment = scalars_end(2, "layer")
    set_moment(1, moment)
    inverse_2 = inverse

    def send_ready(i):
        @pl.when(i > 0)
        def _():
            d = (site + i) % 16
            for q_at in range(4):
                pltpu.make_async_remote_copy(
                    src_ref=chunk3(w_3, d, q_at), dst_ref=chunk2(r_3, mode),
                    send_sem=send_sem.at[2], recv_sem=recv_sem.at[2],
                    device_id=(d, y * 4 + q_at), device_id_type=MESH,
                ).start()

    normalize(w_2, u_2, inverse)
    squares, products = step(2, u_2, u_1, w_3, inverse, send_ready)
    for j in range(1, 4):
        q_at = (q + j) % 4
        pltpu.make_async_remote_copy(
            src_ref=chunk3(w_3, site, q_at), dst_ref=chunk2(r_3, mode),
            send_sem=send_sem.at[2], recv_sem=recv_sem.at[2],
            device_id=(site, y * 4 + q_at), device_id_type=MESH,
        ).start()
    exchange_out_self(2, w_3, r_3).start()
    scalars_start(3, "layer", squares, products)
    scalars_middle(3, "layer", "column")
    exchange_out_wait(1, w_2, r_2)
    finish(r_2, inverse_2, out_2)
    store_2 = pltpu.make_async_copy(out_2, prev, out_sem.at[0])
    store_2.start()
    inverse, moment = scalars_end(3, "column")
    set_moment(2, moment)
    exchange_out_wait(2, w_3, r_3)
    finish(r_3, inverse, out_3)
    store_3 = pltpu.make_async_copy(out_3, last, out_sem.at[1])
    store_3.start()

    for e in range(3):
        wait_send(t.at[pl.ds(0, 63 * 16), :], send_sem.at[e], recv_sem.at[e])
    for r, (group, group_2) in enumerate(
        (("plane", "line"), ("column", "layer"), ("column", "layer"), ("layer", "column"))
    ):
        count, count_2 = groups[group][1], groups[group_2][1]
        wait_send(slots_1.at[r, pl.ds(0, count - 1)], send_1.at[r], recv_1.at[r])
        wait_send(slots_2.at[r, pl.ds(0, count_2 - 1)], send_2.at[r], recv_2.at[r])
    for k, w in enumerate((r_in, w_1, w_2)):
        for copy in halo_copies(k, w):
            copy.wait_send()
    store_2.wait()
    store_3.wait()


def shards(state, operators, op_mask, site_bits, field, site_coupling, mode_coupling):
    block = jax.ShapeDtypeStruct((ROWS, LANES), F32)
    flat = pltpu.VMEM((ROWS, LANES), F32)
    cube = pltpu.VMEM((16, 64, LANES), F32)
    wide = pltpu.VMEM((LANES, ROWS), F32)
    dma = pltpu.SemaphoreType.DMA
    anywhere = pl.BlockSpec(memory_space=pl.ANY)
    hbm = pl.BlockSpec(memory_space=pltpu.HBM)
    scalar = pl.BlockSpec(memory_space=pltpu.SMEM)
    return pl.pallas_call(
        kernel,
        out_shape=(block, block, jax.ShapeDtypeStruct((STEPS,), F32)),
        in_specs=[hbm] * 7,
        out_specs=(anywhere, anywhere, scalar),
        scratch_shapes=[
            pltpu.SMEM((4, 8, 8), jnp.int32),
            pltpu.SMEM((4,), jnp.int32),
            pltpu.SMEM((4,), F32),
            pltpu.SMEM((14,), F32),
            pltpu.SMEM((64,), F32),
            flat,
            pltpu.VMEM((4, ROWS, ROWS), BF16),
            pltpu.VMEM((4, ROWS, ROWS), BF16),
            flat,
            cube,
            flat,
            flat,
            cube,
            cube,
            cube,
            wide,
            wide,
            wide,
            pltpu.VMEM((LANES, ROWS), BF16),
            wide,
            pltpu.VMEM((8, ROWS), F32),
            pltpu.VMEM((3, 2, 16, 8, LANES), F32),
            pltpu.VMEM((4, 64, 1, LANES), F32),
            pltpu.VMEM((4, 16, 1, LANES), F32),
            pltpu.VMEM((4, 1, LANES), F32),
            pltpu.VMEM((4, 1, LANES), F32),
            flat,
            flat,
            dma((7,)),
            dma((3,)),
            dma((2,)),
            dma((3,)),
            dma((3,)),
            dma((3, 2)),
            dma((3, 2)),
            dma((4,)),
            dma((4,)),
            dma((4,)),
            dma((4,)),
        ],
        compiler_params=pltpu.CompilerParams(
            collective_id=0, has_side_effects=True, vmem_limit_bytes=48 * 1024 * 1024
        ),
    )(state, operators, op_mask, site_bits, field, site_coupling, mode_coupling)


def solution(mesh):
    in_specs = (P("site", "phonon"), P(), P(), P(), P(), P(), P())
    out_specs = (P("site", "phonon"), P("site", "phonon"), P())
    return jax.shard_map(shards, mesh=mesh, in_specs=in_specs, out_specs=out_specs, check_vma=False)
```

```python
import functools
import jax
import jax.numpy as jnp
from jax import lax
from jax.experimental import pallas as pl
from jax.experimental.pallas import tpu as pltpu
from jax.sharding import PartitionSpec as P

MESH = pl.DeviceIdType.MESH
F32 = jnp.float32
BF16 = jnp.bfloat16
ROWS = 1024
LANES = 128
STEPS = 3
EPSILON = 1e-06
ENTRIES = 33554432.0


def flipped(value, bit):
    size = 8 << bit
    parts = [value[i * size : (i + 1) * size] for i in range(LANES // size)]
    swapped = []
    for i in range(0, len(parts), 2):
        swapped += [parts[i + 1], parts[i]]
    return jnp.concatenate(swapped, axis=0)


def ring(offset, size):
    return min(offset % size, -offset % size)


def offsets(zs=1, xs=1, ys=1, cores=1):
    found = [
        (dz, dx, dy, dc)
        for dz in range(zs)
        for dx in range(xs)
        for dy in range(ys)
        for dc in range(cores)
        if (dz, dx, dy, dc) != (0, 0, 0, 0)
    ]
    return sorted(found, key=lambda o: -ring(o[0], 8) - ring(o[1], 4) - ring(o[2], 4))


PLANE = offsets(zs=8, xs=4, cores=2)
LINE = offsets(ys=4)
COLUMN = offsets(zs=8, cores=2)
LAYER = offsets(xs=4, ys=4)
WHOLE = offsets(zs=8, xs=4, ys=4, cores=2)


def kernel(
    state, ops, mask_in, site_bits_in, field_in, site_coupling_in, mode_coupling_in,
    last, prev, moments,
    mask, site_bits, field, site_coupling, mode_coupling,
    st, opv, a, t, r_in, r_2, r_3, w_1, w_2, w_3, u_0, u_1, u_2, ub, acc, occ, halo,
    slots_1, slots_2, slots_whole, rows_1, rows_2, out_2, out_3,
    load_sem, self_sem, out_sem, send_sem, recv_sem, hsend_sem, hrecv_sem,
    send_1, recv_1, send_2, recv_2,
):
    site = lax.axis_index("site")
    phonon = lax.axis_index("phonon")
    z_lo, x = site // 4, site % 4
    y, q = phonon // 4, phonon % 4
    z_hi, core = q // 2, q % 2
    z = z_hi * 4 + z_lo
    mode = site * 4 + q

    def place_of(offset):
        dz, dx, dy, dc = offset
        z_at, x_at, y_at, core_at = (z + dz) % 8, (x + dx) % 4, (y + dy) % 4, (core + dc) % 2
        return (z_at % 4) * 4 + x_at, y_at, (z_at // 4) * 2 + core_at

    def device_of(offset):
        site_at, y_at, q_at = place_of(offset)
        return (site_at, y_at * 4 + q_at)

    barrier = pltpu.get_barrier_semaphore()
    for offset in PLANE + LINE:
        pl.semaphore_signal(barrier, inc=1, device_id=device_of(offset), device_id_type=MESH)

    load_state = pltpu.make_async_copy(state, st, load_sem.at[0])
    load_state.start()
    load_ops = pltpu.make_async_copy(ops, opv, load_sem.at[1])
    small = [
        pltpu.make_async_copy(source, target, load_sem.at[2 + i])
        for i, (source, target) in enumerate(
            (
                (mask_in, mask),
                (site_bits_in, site_bits),
                (field_in, field),
                (site_coupling_in, site_coupling),
                (mode_coupling_in, mode_coupling),
            )
        )
    ]
    for copy in small:
        copy.start()
    load_ops.start()

    load_state.wait()
    zero = jnp.zeros((8, LANES), F32)
    squares = zero
    for high in range(8):
        block = st[high * 128 : (high + 1) * 128, :]
        squares = squares + jnp.sum((block * block).reshape(16, 8, LANES), axis=0)
        turned = block.T
        t[pl.ds(high, 64, stride=16), :] = turned[:64]
        t[pl.ds(8 + high, 64, stride=16), :] = turned[64:]

    lane = lax.broadcasted_iota(jnp.int32, (1, LANES), 1)

    def fold(value):
        row = jnp.sum(value, axis=0, keepdims=True)
        return row + pltpu.roll(row, 64, 1)

    def wait_recv(ref, send, recv):
        pltpu.make_async_remote_copy(
            src_ref=ref, dst_ref=ref, send_sem=send, recv_sem=recv,
            device_id=(site, phonon), device_id_type=MESH,
        ).wait_recv()

    def wait_send(ref, send, recv):
        pltpu.make_async_remote_copy(
            src_ref=ref, dst_ref=ref, send_sem=send, recv_sem=recv,
            device_id=(site, phonon), device_id_type=MESH,
        ).wait_send()

    groups = {
        "plane": (PLANE, 64, site * 4 + q),
        "line": (LINE, 4, y),
        "column": (COLUMN, 16, z * 2 + core),
        "layer": (LAYER, 16, x * 4 + y),
        "whole": (WHOLE, 256, site * 16 + phonon),
    }

    def spread(group, src, slots, row, send, recv):
        members, count, index = groups[group]
        src[...] = row
        slots[index] = row
        for offset in members:
            pltpu.make_async_remote_copy(
                src_ref=src, dst_ref=slots.at[index], send_sem=send, recv_sem=recv,
                device_id=device_of(offset), device_id_type=MESH,
            ).start()

    def gather(group, slots, send, recv):
        members, count, index = groups[group]
        wait_recv(slots.at[pl.ds(0, count - 1)], send, recv)
        return jnp.sum(slots[0:count], axis=0)

    def scalars_start(r, group, squares, products):
        row = jnp.where(lane < 64, fold(squares), fold(products))
        spread(group, rows_1.at[r], slots_1.at[r], row, send_1.at[r], recv_1.at[r])

    def scalars_middle(r, group, group_2):
        row = gather(group, slots_1.at[r], send_1.at[r], recv_1.at[r])
        spread(group_2, rows_2.at[r], slots_2.at[r], row, send_2.at[r], recv_2.at[r])

    def scalars_end(r, group_2):
        return measures(gather(group_2, slots_2.at[r], send_2.at[r], recv_2.at[r]))

    def measures(row):
        total = jnp.sum(jnp.where(lane < 64, row, 0.0), axis=1, keepdims=True)
        product = jnp.sum(jnp.where(lane < 64, 0.0, row), axis=1, keepdims=True)
        inverse = 1.0 / jnp.sqrt(total / ENTRIES + EPSILON)
        return inverse, product * inverse / ENTRIES

    def chunk2(ref, i):
        return ref.at[pl.ds(pl.multiple_of(i * 16, 16), 16), :]

    def chunk3(ref, site_at, q_at):
        return ref.at[site_at, pl.ds(pl.multiple_of(q_at * 16, 16), 16), :]

    def exchange_in_self():
        return pltpu.make_async_copy(chunk2(t, mode), chunk3(r_in, site, q), self_sem.at[0])

    def exchange_in_start():
        exchange_in_self().start()
        for offset in PLANE:
            site_at, y_at, q_at = place_of(offset)
            pltpu.make_async_remote_copy(
                src_ref=chunk2(t, site_at * 4 + q_at), dst_ref=chunk3(r_in, site, q),
                send_sem=send_sem.at[0], recv_sem=recv_sem.at[0],
                device_id=(site_at, y_at * 4 + q_at), device_id_type=MESH,
            ).start()

    def exchange_in_wait():
        exchange_in_self().wait()
        wait_recv(t.at[pl.ds(0, 63 * 16), :], send_sem.at[0], recv_sem.at[0])

    def exchange_out_self(e, w, r):
        return pltpu.make_async_copy(chunk3(w, site, q), chunk2(r, mode), self_sem.at[e])

    def exchange_out_start(e, w, r):
        exchange_out_self(e, w, r).start()
        for offset in PLANE:
            site_at, y_at, q_at = place_of(offset)
            pltpu.make_async_remote_copy(
                src_ref=chunk3(w, site_at, q_at), dst_ref=chunk2(r, mode),
                send_sem=send_sem.at[e], recv_sem=recv_sem.at[e],
                device_id=(site_at, y_at * 4 + q_at), device_id_type=MESH,
            ).start()

    def exchange_out_wait(e, w, r):
        exchange_out_self(e, w, r).wait()
        wait_recv(t.at[pl.ds(0, 63 * 16), :], send_sem.at[e], recv_sem.at[e])

    def halo_copies(k, w):
        up = pltpu.make_async_remote_copy(
            src_ref=w.at[:, pl.ds(56, 8), :], dst_ref=halo.at[k, 0],
            send_sem=hsend_sem.at[k, 0], recv_sem=hrecv_sem.at[k, 0],
            device_id=(site, ((y + 1) % 4) * 4 + q), device_id_type=MESH,
        )
        down = pltpu.make_async_remote_copy(
            src_ref=w.at[:, pl.ds(0, 8), :], dst_ref=halo.at[k, 1],
            send_sem=hsend_sem.at[k, 1], recv_sem=hrecv_sem.at[k, 1],
            device_id=(site, ((y + 3) % 4) * 4 + q), device_id_type=MESH,
        )
        return up, down

    pl.semaphore_wait(barrier, 66)
    scalars_start(0, "plane", squares, zero)
    exchange_in_start()

    for copy in small:
        copy.wait()
    chosen = [site_bits[b] for b in range(4)]
    fields = [field[c] for c in chosen]
    device_coupling = [site_coupling[c] for c in chosen]

    place = lax.broadcasted_iota(jnp.int32, (8, ROWS), 1)
    weights = jnp.zeros((8, ROWS), F32)
    for j in range(10):
        weights = weights + site_coupling[4 + j] * ((place >> j) & 1).astype(F32)
    occ[...] = weights

    level = lax.broadcasted_iota(jnp.int32, (8, LANES), 0) + y * 8
    mode_weight = mode_coupling[mode] / jnp.sqrt(F32(32.0))
    lower_weight = mode_weight * jnp.sqrt(level.astype(F32))
    upper_weight = mode_weight * jnp.where(level < 31, jnp.sqrt((level + 1).astype(F32)), 0.0)

    load_ops.wait()

    def mask_operator(b):
        @pl.loop(0, 8)
        def _(i):
            rows = pl.ds(pl.multiple_of(i * 128, 128), 128)
            for j in range(8):
                keep = mask[chosen[b], i, j] > 0
                tile = opv[chosen[b], rows, j * 128 : (j + 1) * 128]
                a[b, j * 128 : (j + 1) * 128, rows] = jnp.where(keep, tile, jnp.zeros_like(tile)).T

    for b in range(4):
        mask_operator(b)
    scalars_middle(0, "plane", "line")
    exchange_in_wait()
    for copy in halo_copies(0, r_in):
        copy.start()
    inverse, _ = scalars_end(0, "line")

    sublane = lax.broadcasted_iota(jnp.int32, (8, LANES), 0)

    def normalize(w, u, inverse):
        scale = jnp.broadcast_to(inverse, (8, LANES))

        @pl.loop(0, 8)
        def _(e):
            for high in range(8):
                cols = slice(high * 128, (high + 1) * 128)
                first = w[2 * e, pl.ds(high, 8, stride=8), :] * scale
                second = w[2 * e + 1, pl.ds(high, 8, stride=8), :] * scale
                both = jnp.concatenate([first, second], axis=0)
                rows = pl.ds(pl.multiple_of(e * 16, 16), 16)
                u[rows, cols] = both
                ub[rows, cols] = both.astype(BF16)

    def step(k, u, u_before, w, inverse, send=None):
        scale = jnp.broadcast_to(inverse, (8, LANES))

        total = None
        for b in range(4):
            product = jnp.dot(ub[...], a[b], preferred_element_type=F32)
            moved = flipped(product + fields[b] * u[...], b)
            total = moved if total is None else total + moved
        acc[...] = total

        for copy in halo_copies(k, w):
            copy.wait_recv()

        def body(i, carry):
            squares, products = carry
            d = (site + 1 + i) % 16
            constant = F32(0.0)
            for b in range(4):
                constant = constant + device_coupling[b] * ((d >> b) & 1).astype(F32)
            rows = pl.ds(pl.multiple_of(d * 8, 8), 8)
            for high in range(8):
                cols = slice(high * 128, (high + 1) * 128)
                here = u[rows, cols]
                below = jnp.broadcast_to(halo[k, 0, d, high : high + 1, :], (8, LANES)) * scale
                above = jnp.broadcast_to(halo[k, 1, d, high : high + 1, :], (8, LANES)) * scale
                lower = jnp.where(sublane == 0, below, pltpu.roll(here, 1, 0))
                upper = jnp.where(sublane == 7, above, pltpu.roll(here, 7, 0))
                ladder = (occ[:, cols] + constant) * (lower_weight * lower + upper_weight * upper)
                new = acc[rows, cols] + ladder
                if k > 0:
                    new = 2.0 * new - u_before[rows, cols] * scale
                w[d, pl.ds(high, 8, stride=8), :] = new
                squares = squares + new * new
                products = products + u_0[rows, cols] * new
            if send is not None:
                send(i)
            return squares, products

        return lax.fori_loop(0, 16, body, (zero, zero))

    def finish(r, inverse, out):
        scale = jnp.broadcast_to(inverse, (128, LANES))
        for high in range(8):
            block = jnp.concatenate(
                [r[pl.ds(high, 64, stride=16), :], r[pl.ds(8 + high, 64, stride=16), :]], axis=0
            )
            out[high * 128 : (high + 1) * 128, :] = block.T * scale

    def set_moment(k, value):
        moments[k] = value[0, 0]

    normalize(r_in, u_0, inverse)
    squares, products = step(0, u_0, u_0, w_1, inverse)
    row = jnp.where(lane < 64, fold(squares), fold(products))
    spread("whole", rows_1.at[1], slots_whole, row, send_1.at[1], recv_1.at[1])
    for copy in halo_copies(1, w_1):
        copy.start()
    inverse, moment = measures(gather("whole", slots_whole, send_1.at[1], recv_1.at[1]))
    set_moment(0, moment)

    normalize(w_1, u_1, inverse)
    squares, products = step(1, u_1, u_0, w_2, inverse)
    scalars_start(2, "column", squares, products)
    for copy in halo_copies(2, w_2):
        copy.start()
    exchange_out_start(1, w_2, r_2)
    scalars_middle(2, "column", "layer")
    inverse, moment = scalars_end(2, "layer")
    set_moment(1, moment)
    inverse_2 = inverse

    def send_ready(i):
        @pl.when(i > 0)
        def _():
            d = (site + i) % 16
            for q_at in range(4):
                pltpu.make_async_remote_copy(
                    src_ref=chunk3(w_3, d, q_at), dst_ref=chunk2(r_3, mode),
                    send_sem=send_sem.at[2], recv_sem=recv_sem.at[2],
                    device_id=(d, y * 4 + q_at), device_id_type=MESH,
                ).start()

    normalize(w_2, u_2, inverse)
    squares, products = step(2, u_2, u_1, w_3, inverse, send_ready)
    for j in range(1, 4):
        q_at = (q + j) % 4
        pltpu.make_async_remote_copy(
            src_ref=chunk3(w_3, site, q_at), dst_ref=chunk2(r_3, mode),
            send_sem=send_sem.at[2], recv_sem=recv_sem.at[2],
            device_id=(site, y * 4 + q_at), device_id_type=MESH,
        ).start()
    exchange_out_self(2, w_3, r_3).start()
    scalars_start(3, "layer", squares, products)
    scalars_middle(3, "layer", "column")
    exchange_out_wait(1, w_2, r_2)
    finish(r_2, inverse_2, out_2)
    store_2 = pltpu.make_async_copy(out_2, prev, out_sem.at[0])
    store_2.start()
    inverse, moment = scalars_end(3, "column")
    set_moment(2, moment)
    exchange_out_wait(2, w_3, r_3)
    finish(r_3, inverse, out_3)
    store_3 = pltpu.make_async_copy(out_3, last, out_sem.at[1])
    store_3.start()

    for e in range(3):
        wait_send(t.at[pl.ds(0, 63 * 16), :], send_sem.at[e], recv_sem.at[e])
    wait_send(slots_whole.at[pl.ds(0, 255)], send_1.at[1], recv_1.at[1])
    for r, group, group_2 in (
        (0, "plane", "line"),
        (2, "column", "layer"),
        (3, "layer", "column"),
    ):
        count, count_2 = groups[group][1], groups[group_2][1]
        wait_send(slots_1.at[r, pl.ds(0, count - 1)], send_1.at[r], recv_1.at[r])
        wait_send(slots_2.at[r, pl.ds(0, count_2 - 1)], send_2.at[r], recv_2.at[r])
    for k, w in enumerate((r_in, w_1, w_2)):
        for copy in halo_copies(k, w):
            copy.wait_send()
    store_2.wait()
    store_3.wait()


def shards(state, operators, op_mask, site_bits, field, site_coupling, mode_coupling):
    block = jax.ShapeDtypeStruct((ROWS, LANES), F32)
    flat = pltpu.VMEM((ROWS, LANES), F32)
    cube = pltpu.VMEM((16, 64, LANES), F32)
    wide = pltpu.VMEM((LANES, ROWS), F32)
    dma = pltpu.SemaphoreType.DMA
    anywhere = pl.BlockSpec(memory_space=pl.ANY)
    hbm = pl.BlockSpec(memory_space=pltpu.HBM)
    scalar = pl.BlockSpec(memory_space=pltpu.SMEM)
    return pl.pallas_call(
        kernel,
        out_shape=(block, block, jax.ShapeDtypeStruct((STEPS,), F32)),
        in_specs=[hbm] * 7,
        out_specs=(anywhere, anywhere, scalar),
        scratch_shapes=[
            pltpu.SMEM((4, 8, 8), jnp.int32),
            pltpu.SMEM((4,), jnp.int32),
            pltpu.SMEM((4,), F32),
            pltpu.SMEM((14,), F32),
            pltpu.SMEM((64,), F32),
            flat,
            pltpu.VMEM((4, ROWS, ROWS), BF16),
            pltpu.VMEM((4, ROWS, ROWS), BF16),
            flat,
            cube,
            flat,
            flat,
            cube,
            cube,
            cube,
            wide,
            wide,
            wide,
            pltpu.VMEM((LANES, ROWS), BF16),
            wide,
            pltpu.VMEM((8, ROWS), F32),
            pltpu.VMEM((3, 2, 16, 8, LANES), F32),
            pltpu.VMEM((4, 64, 1, LANES), F32),
            pltpu.VMEM((4, 16, 1, LANES), F32),
            pltpu.VMEM((256, 1, LANES), F32),
            pltpu.VMEM((4, 1, LANES), F32),
            pltpu.VMEM((4, 1, LANES), F32),
            flat,
            flat,
            dma((7,)),
            dma((3,)),
            dma((2,)),
            dma((3,)),
            dma((3,)),
            dma((3, 2)),
            dma((3, 2)),
            dma((4,)),
            dma((4,)),
            dma((4,)),
            dma((4,)),
        ],
        compiler_params=pltpu.CompilerParams(
            collective_id=0, has_side_effects=True, vmem_limit_bytes=67043328
        ),
    )(state, operators, op_mask, site_bits, field, site_coupling, mode_coupling)


def solution(mesh):
    in_specs = (P("site", "phonon"), P(), P(), P(), P(), P(), P())
    out_specs = (P("site", "phonon"), P("site", "phonon"), P())
    return jax.shard_map(shards, mesh=mesh, in_specs=in_specs, out_specs=out_specs, check_vma=False)
```

```python
import functools
import jax
import jax.numpy as jnp
from jax import lax
from jax.experimental import pallas as pl
from jax.experimental.pallas import tpu as pltpu
from jax.sharding import PartitionSpec as P

MESH = pl.DeviceIdType.MESH
F32 = jnp.float32
BF16 = jnp.bfloat16
ROWS = 1024
LANES = 128
STEPS = 3
EPSILON = 1e-06
ENTRIES = 33554432.0


def flipped(value, bit):
    size = 8 << bit
    parts = [value[i * size : (i + 1) * size] for i in range(LANES // size)]
    swapped = []
    for i in range(0, len(parts), 2):
        swapped += [parts[i + 1], parts[i]]
    return jnp.concatenate(swapped, axis=0)


def ring(offset, size):
    return min(offset % size, -offset % size)


def offsets(zs=1, xs=1, ys=1, cores=1):
    found = [
        (dz, dx, dy, dc)
        for dz in range(zs)
        for dx in range(xs)
        for dy in range(ys)
        for dc in range(cores)
        if (dz, dx, dy, dc) != (0, 0, 0, 0)
    ]
    return sorted(found, key=lambda o: -ring(o[0], 8) - ring(o[1], 4) - ring(o[2], 4))


PLANE = offsets(zs=8, xs=4, cores=2)
LINE = offsets(ys=4)
COLUMN = offsets(zs=8, cores=2)
LAYER = offsets(xs=4, ys=4)
WHOLE = offsets(zs=8, xs=4, ys=4, cores=2)


def kernel(
    state, ops, mask_in, site_bits_in, field_in, site_coupling_in, mode_coupling_in,
    r_3, r_2, stats,
    mask, site_bits, field, site_coupling, mode_coupling,
    st, opv, a, t, r_in, w_1, w_2, w_3, u_0, u_1, u_2, ub, acc, occ, halo,
    slots_1, slots_2, slots_whole, rows_1, rows_2,
    load_sem, self_sem, send_sem, recv_sem, hsend_sem, hrecv_sem,
    send_1, recv_1, send_2, recv_2,
):
    site = lax.axis_index("site")
    phonon = lax.axis_index("phonon")
    z_lo, x = site // 4, site % 4
    y, q = phonon // 4, phonon % 4
    z_hi, core = q // 2, q % 2
    z = z_hi * 4 + z_lo
    mode = site * 4 + q

    def place_of(offset):
        dz, dx, dy, dc = offset
        z_at, x_at, y_at, core_at = (z + dz) % 8, (x + dx) % 4, (y + dy) % 4, (core + dc) % 2
        return (z_at % 4) * 4 + x_at, y_at, (z_at // 4) * 2 + core_at

    def device_of(offset):
        site_at, y_at, q_at = place_of(offset)
        return (site_at, y_at * 4 + q_at)

    barrier = pltpu.get_barrier_semaphore()
    for offset in PLANE + LINE:
        pl.semaphore_signal(barrier, inc=1, device_id=device_of(offset), device_id_type=MESH)

    load_state = pltpu.make_async_copy(state, st, load_sem.at[0])
    load_state.start()
    load_ops = pltpu.make_async_copy(ops, opv, load_sem.at[1])
    small = [
        pltpu.make_async_copy(source, target, load_sem.at[2 + i])
        for i, (source, target) in enumerate(
            (
                (mask_in, mask),
                (site_bits_in, site_bits),
                (field_in, field),
                (site_coupling_in, site_coupling),
                (mode_coupling_in, mode_coupling),
            )
        )
    ]
    for copy in small:
        copy.start()
    load_ops.start()

    load_state.wait()
    zero = jnp.zeros((8, LANES), F32)
    squares = zero
    for high in range(8):
        block = st[high * 128 : (high + 1) * 128, :]
        squares = squares + jnp.sum((block * block).reshape(16, 8, LANES), axis=0)
        turned = block.T
        t[pl.ds(high, 64, stride=16), :] = turned[:64]
        t[pl.ds(8 + high, 64, stride=16), :] = turned[64:]

    lane = lax.broadcasted_iota(jnp.int32, (1, LANES), 1)

    def fold(value):
        row = jnp.sum(value, axis=0, keepdims=True)
        return row + pltpu.roll(row, 64, 1)

    def wait_recv(ref, send, recv):
        pltpu.make_async_remote_copy(
            src_ref=ref, dst_ref=ref, send_sem=send, recv_sem=recv,
            device_id=(site, phonon), device_id_type=MESH,
        ).wait_recv()

    def wait_send(ref, send, recv):
        pltpu.make_async_remote_copy(
            src_ref=ref, dst_ref=ref, send_sem=send, recv_sem=recv,
            device_id=(site, phonon), device_id_type=MESH,
        ).wait_send()

    groups = {
        "plane": (PLANE, 64, site * 4 + q),
        "line": (LINE, 4, y),
        "column": (COLUMN, 16, z * 2 + core),
        "layer": (LAYER, 16, x * 4 + y),
        "whole": (WHOLE, 256, site * 16 + phonon),
    }

    def spread(group, src, slots, row, send, recv):
        members, count, index = groups[group]
        src[...] = row
        slots[index] = row
        for offset in members:
            pltpu.make_async_remote_copy(
                src_ref=src, dst_ref=slots.at[index], send_sem=send, recv_sem=recv,
                device_id=device_of(offset), device_id_type=MESH,
            ).start()

    def gather(group, slots, send, recv):
        members, count, index = groups[group]
        wait_recv(slots.at[pl.ds(0, count - 1)], send, recv)
        return jnp.sum(slots[0:count], axis=0)

    def scalars_start(r, group, squares, products):
        row = jnp.where(lane < 64, fold(squares), fold(products))
        spread(group, rows_1.at[r], slots_1.at[r], row, send_1.at[r], recv_1.at[r])

    def scalars_middle(r, group, group_2):
        row = gather(group, slots_1.at[r], send_1.at[r], recv_1.at[r])
        spread(group_2, rows_2.at[r], slots_2.at[r], row, send_2.at[r], recv_2.at[r])

    def scalars_end(r, group_2):
        return measures(gather(group_2, slots_2.at[r], send_2.at[r], recv_2.at[r]))

    def measures(row):
        total = jnp.sum(jnp.where(lane < 64, row, 0.0), axis=1, keepdims=True)
        product = jnp.sum(jnp.where(lane < 64, 0.0, row), axis=1, keepdims=True)
        inverse = 1.0 / jnp.sqrt(total / ENTRIES + EPSILON)
        return inverse, product * inverse / ENTRIES

    def chunk2(ref, i):
        return ref.at[pl.ds(pl.multiple_of(i * 16, 16), 16), :]

    def chunk3(ref, site_at, q_at):
        return ref.at[site_at, pl.ds(pl.multiple_of(q_at * 16, 16), 16), :]

    def exchange_in_self():
        return pltpu.make_async_copy(chunk2(t, mode), chunk3(r_in, site, q), self_sem.at[0])

    def exchange_in_start():
        exchange_in_self().start()
        for offset in PLANE:
            site_at, y_at, q_at = place_of(offset)
            pltpu.make_async_remote_copy(
                src_ref=chunk2(t, site_at * 4 + q_at), dst_ref=chunk3(r_in, site, q),
                send_sem=send_sem.at[0], recv_sem=recv_sem.at[0],
                device_id=(site_at, y_at * 4 + q_at), device_id_type=MESH,
            ).start()

    def exchange_in_wait():
        exchange_in_self().wait()
        wait_recv(t.at[pl.ds(0, 63 * 16), :], send_sem.at[0], recv_sem.at[0])

    def exchange_out_self(e, w, r):
        return pltpu.make_async_copy(chunk3(w, site, q), chunk2(r, mode), self_sem.at[e])

    def exchange_out_start(e, w, r):
        exchange_out_self(e, w, r).start()
        for offset in PLANE:
            site_at, y_at, q_at = place_of(offset)
            pltpu.make_async_remote_copy(
                src_ref=chunk3(w, site_at, q_at), dst_ref=chunk2(r, mode),
                send_sem=send_sem.at[e], recv_sem=recv_sem.at[e],
                device_id=(site_at, y_at * 4 + q_at), device_id_type=MESH,
            ).start()

    def exchange_out_wait(e, w, r):
        exchange_out_self(e, w, r).wait()
        wait_recv(t.at[pl.ds(0, 63 * 16), :], send_sem.at[e], recv_sem.at[e])

    def halo_copies(k, w):
        up = pltpu.make_async_remote_copy(
            src_ref=w.at[:, pl.ds(56, 8), :], dst_ref=halo.at[k, 0],
            send_sem=hsend_sem.at[k, 0], recv_sem=hrecv_sem.at[k, 0],
            device_id=(site, ((y + 1) % 4) * 4 + q), device_id_type=MESH,
        )
        down = pltpu.make_async_remote_copy(
            src_ref=w.at[:, pl.ds(0, 8), :], dst_ref=halo.at[k, 1],
            send_sem=hsend_sem.at[k, 1], recv_sem=hrecv_sem.at[k, 1],
            device_id=(site, ((y + 3) % 4) * 4 + q), device_id_type=MESH,
        )
        return up, down

    pl.semaphore_wait(barrier, 66)
    scalars_start(0, "plane", squares, zero)
    exchange_in_start()

    for copy in small:
        copy.wait()
    chosen = [site_bits[b] for b in range(4)]
    fields = [field[c] for c in chosen]
    device_coupling = [site_coupling[c] for c in chosen]

    place = lax.broadcasted_iota(jnp.int32, (8, ROWS), 1)
    weights = jnp.zeros((8, ROWS), F32)
    for j in range(10):
        weights = weights + site_coupling[4 + j] * ((place >> j) & 1).astype(F32)
    occ[...] = weights

    level = lax.broadcasted_iota(jnp.int32, (8, LANES), 0) + y * 8
    mode_weight = mode_coupling[mode] / jnp.sqrt(F32(32.0))
    lower_weight = mode_weight * jnp.sqrt(level.astype(F32))
    upper_weight = mode_weight * jnp.where(level < 31, jnp.sqrt((level + 1).astype(F32)), 0.0)

    load_ops.wait()

    def mask_operator(b):
        @pl.loop(0, 8)
        def _(i):
            rows = pl.ds(pl.multiple_of(i * 128, 128), 128)
            for j in range(8):
                keep = mask[chosen[b], i, j] > 0
                tile = opv[chosen[b], rows, j * 128 : (j + 1) * 128]
                a[b, j * 128 : (j + 1) * 128, rows] = jnp.where(keep, tile, jnp.zeros_like(tile)).T

    for b in range(4):
        mask_operator(b)
    scalars_middle(0, "plane", "line")
    exchange_in_wait()
    for copy in halo_copies(0, r_in):
        copy.start()
    inverse, _ = scalars_end(0, "line")

    sublane = lax.broadcasted_iota(jnp.int32, (8, LANES), 0)

    def normalize(w, u, inverse):
        scale = jnp.broadcast_to(inverse, (8, LANES))

        @pl.loop(0, 8)
        def _(e):
            for high in range(8):
                cols = slice(high * 128, (high + 1) * 128)
                first = w[2 * e, pl.ds(high, 8, stride=8), :] * scale
                second = w[2 * e + 1, pl.ds(high, 8, stride=8), :] * scale
                both = jnp.concatenate([first, second], axis=0)
                rows = pl.ds(pl.multiple_of(e * 16, 16), 16)
                u[rows, cols] = both
                ub[rows, cols] = both.astype(BF16)

    def step(k, u, u_before, w, inverse, send=None):
        scale = jnp.broadcast_to(inverse, (8, LANES))

        total = None
        for b in range(4):
            product = jnp.dot(ub[...], a[b], preferred_element_type=F32)
            moved = flipped(product + fields[b] * u[...], b)
            total = moved if total is None else total + moved
        acc[...] = total

        for copy in halo_copies(k, w):
            copy.wait_recv()

        def body(i, carry):
            squares, products = carry
            d = (site + 1 + i) % 16
            constant = F32(0.0)
            for b in range(4):
                constant = constant + device_coupling[b] * ((d >> b) & 1).astype(F32)
            rows = pl.ds(pl.multiple_of(d * 8, 8), 8)
            for high in range(8):
                cols = slice(high * 128, (high + 1) * 128)
                here = u[rows, cols]
                below = jnp.broadcast_to(halo[k, 0, d, high : high + 1, :], (8, LANES)) * scale
                above = jnp.broadcast_to(halo[k, 1, d, high : high + 1, :], (8, LANES)) * scale
                lower = jnp.where(sublane == 0, below, pltpu.roll(here, 1, 0))
                upper = jnp.where(sublane == 7, above, pltpu.roll(here, 7, 0))
                ladder = (occ[:, cols] + constant) * (lower_weight * lower + upper_weight * upper)
                new = acc[rows, cols] + ladder
                if k > 0:
                    new = 2.0 * new - u_before[rows, cols] * scale
                w[d, pl.ds(high, 8, stride=8), :] = new
                squares = squares + new * new
                products = products + u_0[rows, cols] * new
            if send is not None:
                send(i)
            return squares, products

        return lax.fori_loop(0, 16, body, (zero, zero))

    def set_stat(k, value):
        stats[k] = value[0, 0]

    normalize(r_in, u_0, inverse)
    squares, products = step(0, u_0, u_0, w_1, inverse)
    row = jnp.where(lane < 64, fold(squares), fold(products))
    spread("whole", rows_1.at[1], slots_whole, row, send_1.at[1], recv_1.at[1])
    for copy in halo_copies(1, w_1):
        copy.start()
    inverse, moment = measures(gather("whole", slots_whole, send_1.at[1], recv_1.at[1]))
    set_stat(0, moment)

    normalize(w_1, u_1, inverse)
    squares, products = step(1, u_1, u_0, w_2, inverse)
    scalars_start(2, "column", squares, products)
    for copy in halo_copies(2, w_2):
        copy.start()
    exchange_out_start(1, w_2, r_2)
    scalars_middle(2, "column", "layer")
    inverse, moment = scalars_end(2, "layer")
    set_stat(1, moment)
    set_stat(3, inverse)

    def send_ready(i):
        @pl.when(i > 0)
        def _():
            d = (site + i) % 16
            for q_at in range(4):
                pltpu.make_async_remote_copy(
                    src_ref=chunk3(w_3, d, q_at), dst_ref=chunk2(r_3, mode),
                    send_sem=send_sem.at[2], recv_sem=recv_sem.at[2],
                    device_id=(d, y * 4 + q_at), device_id_type=MESH,
                ).start()

    normalize(w_2, u_2, inverse)
    squares, products = step(2, u_2, u_1, w_3, inverse, send_ready)
    for j in range(1, 4):
        q_at = (q + j) % 4
        pltpu.make_async_remote_copy(
            src_ref=chunk3(w_3, site, q_at), dst_ref=chunk2(r_3, mode),
            send_sem=send_sem.at[2], recv_sem=recv_sem.at[2],
            device_id=(site, y * 4 + q_at), device_id_type=MESH,
        ).start()
    exchange_out_self(2, w_3, r_3).start()
    scalars_start(3, "layer", squares, products)
    scalars_middle(3, "layer", "column")
    exchange_out_wait(1, w_2, r_2)
    inverse, moment = scalars_end(3, "column")
    set_stat(2, moment)
    set_stat(4, inverse)
    exchange_out_wait(2, w_3, r_3)

    for e in range(3):
        wait_send(t.at[pl.ds(0, 63 * 16), :], send_sem.at[e], recv_sem.at[e])
    wait_send(slots_whole.at[pl.ds(0, 255)], send_1.at[1], recv_1.at[1])
    for r, group, group_2 in (
        (0, "plane", "line"),
        (2, "column", "layer"),
        (3, "layer", "column"),
    ):
        count, count_2 = groups[group][1], groups[group_2][1]
        wait_send(slots_1.at[r, pl.ds(0, count - 1)], send_1.at[r], recv_1.at[r])
        wait_send(slots_2.at[r, pl.ds(0, count_2 - 1)], send_2.at[r], recv_2.at[r])
    for k, w in enumerate((r_in, w_1, w_2)):
        for copy in halo_copies(k, w):
            copy.wait_send()


def finish_kernel(r_3, r_2, stats, last, prev, moments, v_3, v_2, out_3, out_2, held, kept, sem):
    load = pltpu.make_async_copy(stats, held, sem.at[0])
    load_2 = pltpu.make_async_copy(r_2, v_2, sem.at[1])
    load_3 = pltpu.make_async_copy(r_3, v_3, sem.at[2])
    load.start()
    load_2.start()
    load_3.start()

    def finish(r, scale, out):
        for high in range(8):
            block = jnp.concatenate(
                [r[pl.ds(high, 64, stride=16), :], r[pl.ds(8 + high, 64, stride=16), :]], axis=0
            )
            out[high * 128 : (high + 1) * 128, :] = block.T * scale

    store = pltpu.make_async_copy(kept, moments, sem.at[3])
    store_2 = pltpu.make_async_copy(out_2, prev, sem.at[4])
    store_3 = pltpu.make_async_copy(out_3, last, sem.at[5])
    load.wait()
    for k in range(STEPS):
        kept[k] = held[k]
    store.start()
    load_2.wait()
    finish(v_2, held[3], out_2)
    store_2.start()
    load_3.wait()
    finish(v_3, held[4], out_3)
    store_3.start()
    store.wait()
    store_2.wait()
    store_3.wait()


def shards(state, operators, op_mask, site_bits, field, site_coupling, mode_coupling):
    block = jax.ShapeDtypeStruct((ROWS, LANES), F32)
    flat = pltpu.VMEM((ROWS, LANES), F32)
    cube = pltpu.VMEM((16, 64, LANES), F32)
    wide = pltpu.VMEM((LANES, ROWS), F32)
    dma = pltpu.SemaphoreType.DMA
    hbm = pl.BlockSpec(memory_space=pltpu.HBM)
    scalar = pl.BlockSpec(memory_space=pltpu.SMEM)
    carried = pl.pallas_call(
        kernel,
        out_shape=(block, block, jax.ShapeDtypeStruct((8,), F32)),
        in_specs=[hbm] * 7,
        out_specs=(hbm, hbm, scalar),
        scratch_shapes=[
            pltpu.SMEM((4, 8, 8), jnp.int32),
            pltpu.SMEM((4,), jnp.int32),
            pltpu.SMEM((4,), F32),
            pltpu.SMEM((14,), F32),
            pltpu.SMEM((64,), F32),
            flat,
            pltpu.VMEM((4, ROWS, ROWS), BF16),
            pltpu.VMEM((4, ROWS, ROWS), BF16),
            flat,
            cube,
            cube,
            cube,
            cube,
            wide,
            wide,
            wide,
            pltpu.VMEM((LANES, ROWS), BF16),
            wide,
            pltpu.VMEM((8, ROWS), F32),
            pltpu.VMEM((3, 2, 16, 8, LANES), F32),
            pltpu.VMEM((4, 64, 1, LANES), F32),
            pltpu.VMEM((4, 16, 1, LANES), F32),
            pltpu.VMEM((256, 1, LANES), F32),
            pltpu.VMEM((4, 1, LANES), F32),
            pltpu.VMEM((4, 1, LANES), F32),
            dma((7,)),
            dma((3,)),
            dma((3,)),
            dma((3,)),
            dma((3, 2)),
            dma((3, 2)),
            dma((4,)),
            dma((4,)),
            dma((4,)),
            dma((4,)),
        ],
        compiler_params=pltpu.CompilerParams(
            collective_id=0, has_side_effects=True, vmem_limit_bytes=67043328
        ),
    )(state, operators, op_mask, site_bits, field, site_coupling, mode_coupling)
    return pl.pallas_call(
        finish_kernel,
        out_shape=(block, block, jax.ShapeDtypeStruct((STEPS,), F32)),
        in_specs=[hbm] * 3,
        out_specs=(hbm, hbm, hbm),
        scratch_shapes=[flat] * 4
        + [pltpu.SMEM((8,), F32), pltpu.SMEM((STEPS,), F32), dma((6,))],
        compiler_params=pltpu.CompilerParams(vmem_limit_bytes=67043328),
    )(*carried)


def solution(mesh):
    in_specs = (P("site", "phonon"), P(), P(), P(), P(), P(), P())
    out_specs = (P("site", "phonon"), P("site", "phonon"), P())
    return jax.shard_map(shards, mesh=mesh, in_specs=in_specs, out_specs=out_specs, check_vma=False)
```

```python
import functools
import jax
import jax.numpy as jnp
from jax import lax
from jax.experimental import pallas as pl
from jax.experimental.pallas import tpu as pltpu
from jax.sharding import PartitionSpec as P

MESH = pl.DeviceIdType.MESH
F32 = jnp.float32
BF16 = jnp.bfloat16
ROWS = 1024
LANES = 128
STEPS = 3
EPSILON = 1e-06
ENTRIES = 33554432.0


def flipped(value, bit):
    size = 8 << bit
    parts = [value[i * size : (i + 1) * size] for i in range(LANES // size)]
    swapped = []
    for i in range(0, len(parts), 2):
        swapped += [parts[i + 1], parts[i]]
    return jnp.concatenate(swapped, axis=0)


def ring(offset, size):
    return min(offset % size, -offset % size)


def offsets(zs=1, xs=1, ys=1, cores=1):
    found = [
        (dz, dx, dy, dc)
        for dz in range(zs)
        for dx in range(xs)
        for dy in range(ys)
        for dc in range(cores)
        if (dz, dx, dy, dc) != (0, 0, 0, 0)
    ]
    return sorted(found, key=lambda o: -ring(o[0], 8) - ring(o[1], 4) - ring(o[2], 4))


PLANE = offsets(zs=8, xs=4, cores=2)
LINE = offsets(ys=4)
COLUMN = offsets(zs=8, cores=2)
LAYER = offsets(xs=4, ys=4)
WHOLE = offsets(zs=8, xs=4, ys=4, cores=2)


def kernel(
    state, ops, mask_in, site_bits_in, field_in, site_coupling_in, mode_coupling_in,
    r_3, r_2, stats,
    mask, site_bits, field, site_coupling, mode_coupling,
    st, opv, a, t, r_in, w_1, w_2, w_3, u_0, u_1, ub, acc, linear, occ, halo,
    slots_1, slots_2, slots_whole, rows_1, rows_2,
    load_sem, self_sem, in_sem, send_sem, recv_sem, hsend_sem, hrecv_sem,
    send_1, recv_1, send_2, recv_2,
):
    site = lax.axis_index("site")
    phonon = lax.axis_index("phonon")
    z_lo, x = site // 4, site % 4
    y, q = phonon // 4, phonon % 4
    z_hi, core = q // 2, q % 2
    z = z_hi * 4 + z_lo
    mode = site * 4 + q

    def place_of(offset):
        dz, dx, dy, dc = offset
        z_at, x_at, y_at, core_at = (z + dz) % 8, (x + dx) % 4, (y + dy) % 4, (core + dc) % 2
        return (z_at % 4) * 4 + x_at, y_at, (z_at // 4) * 2 + core_at

    def device_of(offset):
        site_at, y_at, q_at = place_of(offset)
        return (site_at, y_at * 4 + q_at)

    barrier = pltpu.get_barrier_semaphore()
    for offset in PLANE + LINE:
        pl.semaphore_signal(barrier, inc=1, device_id=device_of(offset), device_id_type=MESH)

    load_state = pltpu.make_async_copy(state, st, load_sem.at[0])
    load_state.start()
    load_ops = pltpu.make_async_copy(ops, opv, load_sem.at[1])
    small = [
        pltpu.make_async_copy(source, target, load_sem.at[2 + i])
        for i, (source, target) in enumerate(
            (
                (mask_in, mask),
                (site_bits_in, site_bits),
                (field_in, field),
                (site_coupling_in, site_coupling),
                (mode_coupling_in, mode_coupling),
            )
        )
    ]
    for copy in small:
        copy.start()
    load_ops.start()

    load_state.wait()
    zero = jnp.zeros((8, LANES), F32)
    squares = zero
    for high in range(8):
        block = st[high * 128 : (high + 1) * 128, :]
        squares = squares + jnp.sum((block * block).reshape(16, 8, LANES), axis=0)
        turned = block.T
        t[pl.ds(high, 64, stride=16), :] = turned[:64]
        t[pl.ds(8 + high, 64, stride=16), :] = turned[64:]

    lane = lax.broadcasted_iota(jnp.int32, (1, LANES), 1)

    def fold(value):
        row = jnp.sum(value, axis=0, keepdims=True)
        return row + pltpu.roll(row, 64, 1)

    def wait_recv(ref, send, recv):
        pltpu.make_async_remote_copy(
            src_ref=ref, dst_ref=ref, send_sem=send, recv_sem=recv,
            device_id=(site, phonon), device_id_type=MESH,
        ).wait_recv()

    def wait_send(ref, send, recv):
        pltpu.make_async_remote_copy(
            src_ref=ref, dst_ref=ref, send_sem=send, recv_sem=recv,
            device_id=(site, phonon), device_id_type=MESH,
        ).wait_send()

    groups = {
        "plane": (PLANE, 64, site * 4 + q),
        "line": (LINE, 4, y),
        "column": (COLUMN, 16, z * 2 + core),
        "layer": (LAYER, 16, x * 4 + y),
        "whole": (WHOLE, 256, site * 16 + phonon),
    }

    def spread(group, src, slots, row, send, recv):
        members, count, index = groups[group]
        src[...] = row
        slots[index] = row
        for offset in members:
            pltpu.make_async_remote_copy(
                src_ref=src, dst_ref=slots.at[index], send_sem=send, recv_sem=recv,
                device_id=device_of(offset), device_id_type=MESH,
            ).start()

    def gather(group, slots, send, recv):
        members, count, index = groups[group]
        wait_recv(slots.at[pl.ds(0, count - 1)], send, recv)
        return jnp.sum(slots[0:count], axis=0)

    def scalars_start(r, group, squares, products):
        row = jnp.where(lane < 64, fold(squares), fold(products))
        spread(group, rows_1.at[r], slots_1.at[r], row, send_1.at[r], recv_1.at[r])

    def scalars_middle(r, group, group_2):
        row = gather(group, slots_1.at[r], send_1.at[r], recv_1.at[r])
        spread(group_2, rows_2.at[r], slots_2.at[r], row, send_2.at[r], recv_2.at[r])

    def scalars_end(r, group_2):
        return measures(gather(group_2, slots_2.at[r], send_2.at[r], recv_2.at[r]))

    def measures(row):
        total = jnp.sum(jnp.where(lane < 64, row, 0.0), axis=1, keepdims=True)
        product = jnp.sum(jnp.where(lane < 64, 0.0, row), axis=1, keepdims=True)
        inverse = 1.0 / jnp.sqrt(total / ENTRIES + EPSILON)
        return inverse, product * inverse / ENTRIES

    def chunk2(ref, i):
        return ref.at[pl.ds(pl.multiple_of(i * 16, 16), 16), :]

    def chunk3(ref, site_at, q_at):
        return ref.at[site_at, pl.ds(pl.multiple_of(q_at * 16, 16), 16), :]

    early = (q == 0) | (q == 3)
    kind = jnp.where(early, 0, 1)

    def exchange_in_start():
        pltpu.make_async_copy(chunk2(t, mode), chunk3(r_in, site, q), in_sem.at[kind]).start()
        for offset in PLANE:
            site_at, y_at, q_at = place_of(offset)
            pltpu.make_async_remote_copy(
                src_ref=chunk2(t, site_at * 4 + q_at), dst_ref=chunk3(r_in, site, q),
                send_sem=send_sem.at[0], recv_sem=in_sem.at[kind],
                device_id=(site_at, y_at * 4 + q_at), device_id_type=MESH,
            ).start()

    def exchange_in_wait(which):
        wait_recv(t.at[pl.ds(0, 32 * 16), :], send_sem.at[0], in_sem.at[which])

    def exchange_out_self(e, w, r):
        return pltpu.make_async_copy(chunk3(w, site, q), chunk2(r, mode), self_sem.at[e])

    def exchange_out_start(e, w, r):
        exchange_out_self(e, w, r).start()
        for offset in PLANE:
            site_at, y_at, q_at = place_of(offset)
            pltpu.make_async_remote_copy(
                src_ref=chunk3(w, site_at, q_at), dst_ref=chunk2(r, mode),
                send_sem=send_sem.at[e], recv_sem=recv_sem.at[e],
                device_id=(site_at, y_at * 4 + q_at), device_id_type=MESH,
            ).start()

    def exchange_out_wait(e, w, r):
        exchange_out_self(e, w, r).wait()
        wait_recv(t.at[pl.ds(0, 63 * 16), :], send_sem.at[e], recv_sem.at[e])

    def halo_copies(k, w):
        up = pltpu.make_async_remote_copy(
            src_ref=w.at[:, pl.ds(56, 8), :], dst_ref=halo.at[k, 0],
            send_sem=hsend_sem.at[k, 0], recv_sem=hrecv_sem.at[k, 0],
            device_id=(site, ((y + 1) % 4) * 4 + q), device_id_type=MESH,
        )
        down = pltpu.make_async_remote_copy(
            src_ref=w.at[:, pl.ds(0, 8), :], dst_ref=halo.at[k, 1],
            send_sem=hsend_sem.at[k, 1], recv_sem=hrecv_sem.at[k, 1],
            device_id=(site, ((y + 3) % 4) * 4 + q), device_id_type=MESH,
        )
        return up, down

    pl.semaphore_wait(barrier, 66)
    scalars_start(0, "plane", squares, zero)
    pl.when(early)(exchange_in_start)

    for copy in small:
        copy.wait()
    chosen = [site_bits[b] for b in range(4)]
    fields = [field[c] for c in chosen]
    device_coupling = [site_coupling[c] for c in chosen]

    place = lax.broadcasted_iota(jnp.int32, (8, ROWS), 1)
    weights = jnp.zeros((8, ROWS), F32)
    for j in range(10):
        weights = weights + site_coupling[4 + j] * ((place >> j) & 1).astype(F32)
    occ[...] = weights

    level = lax.broadcasted_iota(jnp.int32, (8, LANES), 0) + y * 8
    mode_weight = mode_coupling[mode] / jnp.sqrt(F32(32.0))
    lower_weight = mode_weight * jnp.sqrt(level.astype(F32))
    upper_weight = mode_weight * jnp.where(level < 31, jnp.sqrt((level + 1).astype(F32)), 0.0)

    load_ops.wait()

    def mask_operator(b):
        @pl.loop(0, 8)
        def _(i):
            rows = pl.ds(pl.multiple_of(i * 128, 128), 128)
            for j in range(8):
                keep = mask[chosen[b], i, j] > 0
                tile = opv[chosen[b], rows, j * 128 : (j + 1) * 128]
                a[b, j * 128 : (j + 1) * 128, rows] = jnp.where(keep, tile, jnp.zeros_like(tile)).T

    for b in range(4):
        mask_operator(b)
    pl.when(jnp.logical_not(early))(exchange_in_start)
    scalars_middle(0, "plane", "line")
    exchange_in_wait(0)
    for copy in halo_copies(0, r_in):
        copy.start()
    exchange_in_wait(1)
    inverse, _ = scalars_end(0, "line")

    sublane = lax.broadcasted_iota(jnp.int32, (8, LANES), 0)

    def normalize(w, u, inverse):
        scale = jnp.broadcast_to(inverse, (8, LANES))

        @pl.loop(0, 8)
        def _(e):
            for high in range(8):
                cols = slice(high * 128, (high + 1) * 128)
                first = w[2 * e, pl.ds(high, 8, stride=8), :] * scale
                second = w[2 * e + 1, pl.ds(high, 8, stride=8), :] * scale
                both = jnp.concatenate([first, second], axis=0)
                rows = pl.ds(pl.multiple_of(e * 16, 16), 16)
                if u is not None:
                    u[rows, cols] = both
                ub[rows, cols] = both.astype(BF16)

    def bits_of(d):
        return [(d // (1 << b)) % 2 for b in range(4)]

    def ladder_of(k, d, high, here):
        cols = slice(high * 128, (high + 1) * 128)
        constant = F32(0.0)
        for b, bit in enumerate(bits_of(d)):
            constant = constant + device_coupling[b] * bit.astype(F32)
        below = jnp.broadcast_to(halo[k, 0, d, high : high + 1, :], (8, LANES))
        above = jnp.broadcast_to(halo[k, 1, d, high : high + 1, :], (8, LANES))
        lower = jnp.where(sublane == 0, below, pltpu.roll(here, 1, 0))
        upper = jnp.where(sublane == 7, above, pltpu.roll(here, 7, 0))
        return (occ[:, cols] + constant) * (lower_weight * lower + upper_weight * upper)

    def prepare(k, w_before, w):
        for copy in halo_copies(k, w):
            copy.wait_recv()

        @pl.loop(0, 16)
        def _(d):
            bits = bits_of(d)
            rows = pl.ds(pl.multiple_of(d * 8, 8), 8)
            for high in range(8):
                cols = slice(high * 128, (high + 1) * 128)
                here = w_before[d, pl.ds(high, 8, stride=8), :]
                value = ladder_of(k, d, high, here)
                for b in range(4):
                    other = d + (1 - 2 * bits[b]) * (1 << b)
                    value = value + fields[b] * w_before[other, pl.ds(high, 8, stride=8), :]
                linear[rows, cols] = value

    def multiply():
        total = None
        for b in range(4):
            product = flipped(jnp.dot(ub[...], a[b], preferred_element_type=F32), b)
            total = product if total is None else total + product
        acc[...] = total

    def combine(k, u_before, w, inverse, send=None):
        scale = jnp.broadcast_to(inverse, (8, LANES))

        def body(i, carry):
            squares, products = carry
            d = (site + 1 + i) % 16
            rows = pl.ds(pl.multiple_of(d * 8, 8), 8)
            for high in range(8):
                cols = slice(high * 128, (high + 1) * 128)
                new = acc[rows, cols] + linear[rows, cols] * scale
                if k > 0:
                    new = 2.0 * new - u_before[rows, cols] * scale
                w[d, pl.ds(high, 8, stride=8), :] = new
                squares = squares + new * new
                products = products + u_0[rows, cols] * new
            if send is not None:
                send(i)
            return squares, products

        return lax.fori_loop(0, 16, body, (zero, zero))

    def set_stat(k, value):
        stats[k] = value[0, 0]

    normalize(r_in, u_0, inverse)
    multiply()
    prepare(0, r_in, w_1)
    squares, products = combine(0, None, w_1, inverse)
    row = jnp.where(lane < 64, fold(squares), fold(products))
    spread("whole", rows_1.at[1], slots_whole, row, send_1.at[1], recv_1.at[1])
    for copy in halo_copies(1, w_1):
        copy.start()
    prepare(1, w_1, w_2)
    inverse, moment = measures(gather("whole", slots_whole, send_1.at[1], recv_1.at[1]))
    set_stat(0, moment)

    normalize(w_1, u_1, inverse)
    multiply()
    squares, products = combine(1, u_0, w_2, inverse)
    scalars_start(2, "column", squares, products)
    for copy in halo_copies(2, w_2):
        copy.start()
    exchange_out_start(1, w_2, r_2)
    prepare(2, w_2, w_3)
    scalars_middle(2, "column", "layer")
    inverse, moment = scalars_end(2, "layer")
    set_stat(1, moment)
    set_stat(3, inverse)

    def send_ready(i):
        @pl.when(i > 0)
        def _():
            d = (site + i) % 16
            for q_at in range(4):
                pltpu.make_async_remote_copy(
                    src_ref=chunk3(w_3, d, q_at), dst_ref=chunk2(r_3, mode),
                    send_sem=send_sem.at[2], recv_sem=recv_sem.at[2],
                    device_id=(d, y * 4 + q_at), device_id_type=MESH,
                ).start()

    normalize(w_2, None, inverse)
    multiply()
    squares, products = combine(2, u_1, w_3, inverse, send_ready)
    for j in range(1, 4):
        q_at = (q + j) % 4
        pltpu.make_async_remote_copy(
            src_ref=chunk3(w_3, site, q_at), dst_ref=chunk2(r_3, mode),
            send_sem=send_sem.at[2], recv_sem=recv_sem.at[2],
            device_id=(site, y * 4 + q_at), device_id_type=MESH,
        ).start()
    exchange_out_self(2, w_3, r_3).start()
    scalars_start(3, "layer", squares, products)
    scalars_middle(3, "layer", "column")
    exchange_out_wait(1, w_2, r_2)
    inverse, moment = scalars_end(3, "column")
    set_stat(2, moment)
    set_stat(4, inverse)
    exchange_out_wait(2, w_3, r_3)

    for e in range(3):
        wait_send(t.at[pl.ds(0, 63 * 16), :], send_sem.at[e], recv_sem.at[e])
    wait_send(slots_whole.at[pl.ds(0, 255)], send_1.at[1], recv_1.at[1])
    for r, group, group_2 in (
        (0, "plane", "line"),
        (2, "column", "layer"),
        (3, "layer", "column"),
    ):
        count, count_2 = groups[group][1], groups[group_2][1]
        wait_send(slots_1.at[r, pl.ds(0, count - 1)], send_1.at[r], recv_1.at[r])
        wait_send(slots_2.at[r, pl.ds(0, count_2 - 1)], send_2.at[r], recv_2.at[r])
    for k, w in enumerate((r_in, w_1, w_2)):
        for copy in halo_copies(k, w):
            copy.wait_send()


def finish_kernel(r_3, r_2, stats, last, prev, moments, v_3, v_2, out_3, out_2, held, kept, sem, store_sem):
    load = pltpu.make_async_copy(stats, held, sem.at[0])
    load_2 = pltpu.make_async_copy(r_2, v_2, sem.at[1])
    load_3 = pltpu.make_async_copy(r_3, v_3, sem.at[2])
    load.start()
    load_2.start()
    load_3.start()

    def finish(r, scale, out, stores):
        for high in range(8):
            block = jnp.concatenate(
                [r[pl.ds(high, 64, stride=16), :], r[pl.ds(8 + high, 64, stride=16), :]], axis=0
            )
            out[high * 128 : (high + 1) * 128, :] = block.T * scale
            stores[high].start()

    def stores_of(out, result, k):
        return [
            pltpu.make_async_copy(
                out.at[pl.ds(high * 128, 128), :], result.at[pl.ds(high * 128, 128), :], store_sem.at[k, high]
            )
            for high in range(8)
        ]

    store = pltpu.make_async_copy(kept, moments, sem.at[3])
    stores_2 = stores_of(out_2, prev, 0)
    stores_3 = stores_of(out_3, last, 1)
    load.wait()
    for k in range(STEPS):
        kept[k] = held[k]
    store.start()
    load_2.wait()
    finish(v_2, held[3], out_2, stores_2)
    load_3.wait()
    finish(v_3, held[4], out_3, stores_3)
    store.wait()
    for copy in stores_2 + stores_3:
        copy.wait()


def shards(state, operators, op_mask, site_bits, field, site_coupling, mode_coupling):
    block = jax.ShapeDtypeStruct((ROWS, LANES), F32)
    flat = pltpu.VMEM((ROWS, LANES), F32)
    cube = pltpu.VMEM((16, 64, LANES), F32)
    wide = pltpu.VMEM((LANES, ROWS), F32)
    dma = pltpu.SemaphoreType.DMA
    hbm = pl.BlockSpec(memory_space=pltpu.HBM)
    scalar = pl.BlockSpec(memory_space=pltpu.SMEM)
    carried = pl.pallas_call(
        kernel,
        out_shape=(block, block, jax.ShapeDtypeStruct((8,), F32)),
        in_specs=[hbm] * 7,
        out_specs=(hbm, hbm, scalar),
        scratch_shapes=[
            pltpu.SMEM((4, 8, 8), jnp.int32),
            pltpu.SMEM((4,), jnp.int32),
            pltpu.SMEM((4,), F32),
            pltpu.SMEM((14,), F32),
            pltpu.SMEM((64,), F32),
            flat,
            pltpu.VMEM((4, ROWS, ROWS), BF16),
            pltpu.VMEM((4, ROWS, ROWS), BF16),
            flat,
            cube,
            cube,
            cube,
            cube,
            wide,
            wide,
            pltpu.VMEM((LANES, ROWS), BF16),
            wide,
            wide,
            pltpu.VMEM((8, ROWS), F32),
            pltpu.VMEM((3, 2, 16, 8, LANES), F32),
            pltpu.VMEM((4, 64, 1, LANES), F32),
            pltpu.VMEM((4, 16, 1, LANES), F32),
            pltpu.VMEM((256, 1, LANES), F32),
            pltpu.VMEM((4, 1, LANES), F32),
            pltpu.VMEM((4, 1, LANES), F32),
            dma((7,)),
            dma((3,)),
            dma((2,)),
            dma((3,)),
            dma((3,)),
            dma((3, 2)),
            dma((3, 2)),
            dma((4,)),
            dma((4,)),
            dma((4,)),
            dma((4,)),
        ],
        compiler_params=pltpu.CompilerParams(
            collective_id=0, has_side_effects=True, vmem_limit_bytes=67043328
        ),
    )(state, operators, op_mask, site_bits, field, site_coupling, mode_coupling)
    return pl.pallas_call(
        finish_kernel,
        out_shape=(block, block, jax.ShapeDtypeStruct((STEPS,), F32)),
        in_specs=[hbm] * 3,
        out_specs=(hbm, hbm, hbm),
        scratch_shapes=[flat] * 4
        + [pltpu.SMEM((8,), F32), pltpu.SMEM((STEPS,), F32), dma((4,)), dma((2, 8))],
        compiler_params=pltpu.CompilerParams(vmem_limit_bytes=67043328),
    )(*carried)


def solution(mesh):
    in_specs = (P("site", "phonon"), P(), P(), P(), P(), P(), P())
    out_specs = (P("site", "phonon"), P("site", "phonon"), P())
    return jax.shard_map(shards, mesh=mesh, in_specs=in_specs, out_specs=out_specs, check_vma=False)
```

```python
import functools
import jax
import jax.numpy as jnp
from jax import lax
from jax.experimental import pallas as pl
from jax.experimental.pallas import tpu as pltpu
from jax.sharding import PartitionSpec as P

MESH = pl.DeviceIdType.MESH
F32 = jnp.float32
BF16 = jnp.bfloat16
ROWS = 1024
LANES = 128
STEPS = 3
EPSILON = 1e-06
ENTRIES = 33554432.0


def flipped(value, bit):
    size = 8 << bit
    parts = [value[i * size : (i + 1) * size] for i in range(LANES // size)]
    swapped = []
    for i in range(0, len(parts), 2):
        swapped += [parts[i + 1], parts[i]]
    return jnp.concatenate(swapped, axis=0)


def ring(offset, size):
    return min(offset % size, -offset % size)


def offsets(zs=1, xs=1, ys=1, cores=1):
    found = [
        (dz, dx, dy, dc)
        for dz in range(zs)
        for dx in range(xs)
        for dy in range(ys)
        for dc in range(cores)
        if (dz, dx, dy, dc) != (0, 0, 0, 0)
    ]
    return sorted(found, key=lambda o: -ring(o[0], 8) - ring(o[1], 4) - ring(o[2], 4))


PLANE = offsets(zs=8, xs=4, cores=2)
LINE = offsets(ys=4)
COLUMN = offsets(zs=8, cores=2)
LAYER = offsets(xs=4, ys=4)
WHOLE = offsets(zs=8, xs=4, ys=4, cores=2)


def kernel(
    state, ops, mask_in, site_bits_in, field_in, site_coupling_in, mode_coupling_in,
    r_3, r_2, stats,
    mask, site_bits, field, site_coupling, mode_coupling,
    st, opv, a, t, r_in, w_1, w_2, w_3, u_0, u_1, ub, acc, linear, occ, halo,
    slots_1, slots_2, slots_whole, rows_1, rows_2,
    load_sem, self_sem, in_sem, send_sem, recv_sem, hsend_sem, hrecv_sem,
    send_1, recv_1, send_2, recv_2,
):
    site = lax.axis_index("site")
    phonon = lax.axis_index("phonon")
    z_lo, x = site // 4, site % 4
    y, q = phonon // 4, phonon % 4
    z_hi, core = q // 2, q % 2
    z = z_hi * 4 + z_lo
    mode = site * 4 + q

    def place_of(offset):
        dz, dx, dy, dc = offset
        z_at, x_at, y_at, core_at = (z + dz) % 8, (x + dx) % 4, (y + dy) % 4, (core + dc) % 2
        return (z_at % 4) * 4 + x_at, y_at, (z_at // 4) * 2 + core_at

    def device_of(offset):
        site_at, y_at, q_at = place_of(offset)
        return (site_at, y_at * 4 + q_at)

    barrier = pltpu.get_barrier_semaphore()
    for offset in PLANE + LINE:
        pl.semaphore_signal(barrier, inc=1, device_id=device_of(offset), device_id_type=MESH)

    load_state = pltpu.make_async_copy(state, st, load_sem.at[0])
    load_state.start()
    load_ops = pltpu.make_async_copy(ops, opv, load_sem.at[1])
    small = [
        pltpu.make_async_copy(source, target, load_sem.at[2 + i])
        for i, (source, target) in enumerate(
            (
                (mask_in, mask),
                (site_bits_in, site_bits),
                (field_in, field),
                (site_coupling_in, site_coupling),
                (mode_coupling_in, mode_coupling),
            )
        )
    ]
    for copy in small:
        copy.start()
    load_ops.start()

    load_state.wait()
    zero = jnp.zeros((8, LANES), F32)
    squares = zero
    for high in range(8):
        block = st[high * 128 : (high + 1) * 128, :]
        squares = squares + jnp.sum((block * block).reshape(16, 8, LANES), axis=0)
        turned = block.T
        t[pl.ds(high, 64, stride=16), :] = turned[:64]
        t[pl.ds(8 + high, 64, stride=16), :] = turned[64:]

    lane = lax.broadcasted_iota(jnp.int32, (1, LANES), 1)

    def fold(value):
        row = jnp.sum(value, axis=0, keepdims=True)
        return row + pltpu.roll(row, 64, 1)

    def wait_recv(ref, send, recv):
        pltpu.make_async_remote_copy(
            src_ref=ref, dst_ref=ref, send_sem=send, recv_sem=recv,
            device_id=(site, phonon), device_id_type=MESH,
        ).wait_recv()

    def wait_send(ref, send, recv):
        pltpu.make_async_remote_copy(
            src_ref=ref, dst_ref=ref, send_sem=send, recv_sem=recv,
            device_id=(site, phonon), device_id_type=MESH,
        ).wait_send()

    groups = {
        "plane": (PLANE, 64, site * 4 + q),
        "line": (LINE, 4, y),
        "column": (COLUMN, 16, z * 2 + core),
        "layer": (LAYER, 16, x * 4 + y),
        "whole": (WHOLE, 256, site * 16 + phonon),
    }

    def spread(group, src, slots, row, send, recv):
        members, count, index = groups[group]
        src[...] = row
        slots[index] = row
        for offset in members:
            pltpu.make_async_remote_copy(
                src_ref=src, dst_ref=slots.at[index], send_sem=send, recv_sem=recv,
                device_id=device_of(offset), device_id_type=MESH,
            ).start()

    def gather(group, slots, send, recv):
        members, count, index = groups[group]
        wait_recv(slots.at[pl.ds(0, count - 1)], send, recv)
        return jnp.sum(slots[0:count], axis=0)

    def scalars_start(r, group, squares, products):
        row = jnp.where(lane < 64, fold(squares), fold(products))
        spread(group, rows_1.at[r], slots_1.at[r], row, send_1.at[r], recv_1.at[r])

    def scalars_middle(r, group, group_2):
        row = gather(group, slots_1.at[r], send_1.at[r], recv_1.at[r])
        spread(group_2, rows_2.at[r], slots_2.at[r], row, send_2.at[r], recv_2.at[r])

    def scalars_end(r, group_2):
        return measures(gather(group_2, slots_2.at[r], send_2.at[r], recv_2.at[r]))

    def measures(row):
        total = jnp.sum(jnp.where(lane < 64, row, 0.0), axis=1, keepdims=True)
        product = jnp.sum(jnp.where(lane < 64, 0.0, row), axis=1, keepdims=True)
        inverse = 1.0 / jnp.sqrt(total / ENTRIES + EPSILON)
        return inverse, product * inverse / ENTRIES

    def chunk2(ref, i):
        return ref.at[pl.ds(pl.multiple_of(i * 16, 16), 16), :]

    def chunk3(ref, site_at, q_at):
        return ref.at[site_at, pl.ds(pl.multiple_of(q_at * 16, 16), 16), :]

    early = (q == 0) | (q == 3)
    kind = jnp.where(early, 0, 1)

    def exchange_in_start():
        pltpu.make_async_copy(chunk2(t, mode), chunk3(r_in, site, q), in_sem.at[kind]).start()
        for offset in PLANE:
            site_at, y_at, q_at = place_of(offset)
            pltpu.make_async_remote_copy(
                src_ref=chunk2(t, site_at * 4 + q_at), dst_ref=chunk3(r_in, site, q),
                send_sem=send_sem.at[0], recv_sem=in_sem.at[kind],
                device_id=(site_at, y_at * 4 + q_at), device_id_type=MESH,
            ).start()

    def exchange_in_wait(which):
        wait_recv(t.at[pl.ds(0, 32 * 16), :], send_sem.at[0], in_sem.at[which])

    def exchange_out_self(e, w, r):
        return pltpu.make_async_copy(chunk3(w, site, q), chunk2(r, mode), self_sem.at[e])

    def exchange_out_start(e, w, r):
        exchange_out_self(e, w, r).start()
        for offset in PLANE:
            site_at, y_at, q_at = place_of(offset)
            pltpu.make_async_remote_copy(
                src_ref=chunk3(w, site_at, q_at), dst_ref=chunk2(r, mode),
                send_sem=send_sem.at[e], recv_sem=recv_sem.at[e],
                device_id=(site_at, y_at * 4 + q_at), device_id_type=MESH,
            ).start()

    def exchange_out_wait(e, w, r):
        exchange_out_self(e, w, r).wait()
        wait_recv(t.at[pl.ds(0, 63 * 16), :], send_sem.at[e], recv_sem.at[e])

    def halo_copies(k, w):
        up = pltpu.make_async_remote_copy(
            src_ref=w.at[:, pl.ds(56, 8), :], dst_ref=halo.at[k, 0],
            send_sem=hsend_sem.at[k, 0], recv_sem=hrecv_sem.at[k, 0],
            device_id=(site, ((y + 1) % 4) * 4 + q), device_id_type=MESH,
        )
        down = pltpu.make_async_remote_copy(
            src_ref=w.at[:, pl.ds(0, 8), :], dst_ref=halo.at[k, 1],
            send_sem=hsend_sem.at[k, 1], recv_sem=hrecv_sem.at[k, 1],
            device_id=(site, ((y + 3) % 4) * 4 + q), device_id_type=MESH,
        )
        return up, down

    pl.semaphore_wait(barrier, 66)
    scalars_start(0, "plane", squares, zero)
    pl.when(early)(exchange_in_start)

    for copy in small:
        copy.wait()
    chosen = [site_bits[b] for b in range(4)]
    fields = [field[c] for c in chosen]
    device_coupling = [site_coupling[c] for c in chosen]

    place = lax.broadcasted_iota(jnp.int32, (8, ROWS), 1)
    weights = jnp.zeros((8, ROWS), F32)
    for j in range(10):
        weights = weights + site_coupling[4 + j] * ((place >> j) & 1).astype(F32)
    occ[...] = weights

    level = lax.broadcasted_iota(jnp.int32, (8, LANES), 0) + y * 8
    mode_weight = mode_coupling[mode] / jnp.sqrt(F32(32.0))
    lower_weight = mode_weight * jnp.sqrt(level.astype(F32))
    upper_weight = mode_weight * jnp.where(level < 31, jnp.sqrt((level + 1).astype(F32)), 0.0)

    load_ops.wait()

    def mask_operator(b):
        @pl.loop(0, 8)
        def _(i):
            rows = pl.ds(pl.multiple_of(i * 128, 128), 128)
            for j in range(8):
                keep = mask[chosen[b], i, j] > 0
                tile = opv[chosen[b], rows, j * 128 : (j + 1) * 128]
                a[b, j * 128 : (j + 1) * 128, rows] = jnp.where(keep, tile, jnp.zeros_like(tile)).T

    for b in range(4):
        mask_operator(b)
    pl.when(jnp.logical_not(early))(exchange_in_start)
    scalars_middle(0, "plane", "line")
    exchange_in_wait(0)
    for copy in halo_copies(0, r_in):
        copy.start()
    exchange_in_wait(1)
    inverse, _ = scalars_end(0, "line")

    sublane = lax.broadcasted_iota(jnp.int32, (8, LANES), 0)

    def normalize(w, u, inverse):
        scale = jnp.broadcast_to(inverse, (8, LANES))

        @pl.loop(0, 8)
        def _(e):
            for high in range(8):
                cols = slice(high * 128, (high + 1) * 128)
                first = w[2 * e, pl.ds(high, 8, stride=8), :] * scale
                second = w[2 * e + 1, pl.ds(high, 8, stride=8), :] * scale
                both = jnp.concatenate([first, second], axis=0)
                rows = pl.ds(pl.multiple_of(e * 16, 16), 16)
                if u is not None:
                    u[rows, cols] = both
                ub[rows, cols] = both.astype(BF16)

    def bits_of(d):
        if isinstance(d, int):
            return [jnp.int32((d >> b) & 1) for b in range(4)]
        return [(d // (1 << b)) % 2 for b in range(4)]

    def ladder_of(k, d, high, here):
        cols = slice(high * 128, (high + 1) * 128)
        constant = F32(0.0)
        for b, bit in enumerate(bits_of(d)):
            constant = constant + device_coupling[b] * bit.astype(F32)
        below = jnp.broadcast_to(halo[k, 0, d, high : high + 1, :], (8, LANES))
        above = jnp.broadcast_to(halo[k, 1, d, high : high + 1, :], (8, LANES))
        lower = jnp.where(sublane == 0, below, pltpu.roll(here, 1, 0))
        upper = jnp.where(sublane == 7, above, pltpu.roll(here, 7, 0))
        return (occ[:, cols] + constant) * (lower_weight * lower + upper_weight * upper)

    def prepare(k, w_before, w):
        for copy in halo_copies(k, w):
            copy.wait_recv()

        @pl.loop(0, 16)
        def _(d):
            bits = bits_of(d)
            rows = pl.ds(pl.multiple_of(d * 8, 8), 8)
            for high in range(8):
                cols = slice(high * 128, (high + 1) * 128)
                here = w_before[d, pl.ds(high, 8, stride=8), :]
                value = ladder_of(k, d, high, here)
                for b in range(4):
                    other = d + (1 - 2 * bits[b]) * (1 << b)
                    value = value + fields[b] * w_before[other, pl.ds(high, 8, stride=8), :]
                linear[rows, cols] = value

    def linear_part(w_before, k, d, high):
        value = ladder_of(k, d, high, w_before[d, pl.ds(high, 8, stride=8), :])
        for b in range(4):
            value = value + fields[b] * w_before[d ^ (1 << b), pl.ds(high, 8, stride=8), :]
        return value

    def step(k, u_before, w_before, w, inverse, part):
        scale = jnp.broadcast_to(inverse, (8, LANES))
        total = None
        for b in range(4):
            product = flipped(jnp.dot(ub[...], a[b], preferred_element_type=F32), b)
            total = product if total is None else total + product
        squares, products = zero, zero
        for d in range(16):
            rows = slice(d * 8, (d + 1) * 8)
            for high in range(8):
                cols = slice(high * 128, (high + 1) * 128)
                new = total[rows, cols] + part(d, high) * scale
                if k > 0:
                    new = 2.0 * new - u_before[rows, cols] * scale
                w[d, pl.ds(high, 8, stride=8), :] = new
                squares = squares + new * new
                products = products + u_0[rows, cols] * new
        return squares, products

    def multiply():
        total = None
        for b in range(4):
            product = flipped(jnp.dot(ub[...], a[b], preferred_element_type=F32), b)
            total = product if total is None else total + product
        acc[...] = total

    def combine(k, u_before, w, inverse, send=None):
        scale = jnp.broadcast_to(inverse, (8, LANES))

        def body(i, carry):
            squares, products = carry
            d = (site + 1 + i) % 16
            rows = pl.ds(pl.multiple_of(d * 8, 8), 8)
            for high in range(8):
                cols = slice(high * 128, (high + 1) * 128)
                new = acc[rows, cols] + linear[rows, cols] * scale
                if k > 0:
                    new = 2.0 * new - u_before[rows, cols] * scale
                w[d, pl.ds(high, 8, stride=8), :] = new
                squares = squares + new * new
                products = products + u_0[rows, cols] * new
            if send is not None:
                send(i)
            return squares, products

        return lax.fori_loop(0, 16, body, (zero, zero))

    def set_stat(k, value):
        stats[k] = value[0, 0]

    normalize(r_in, u_0, inverse)
    for copy in halo_copies(0, r_in):
        copy.wait_recv()
    squares, products = step(
        0, None, r_in, w_1, inverse, lambda d, high: linear_part(r_in, 0, d, high)
    )
    row = jnp.where(lane < 64, fold(squares), fold(products))
    spread("whole", rows_1.at[1], slots_whole, row, send_1.at[1], recv_1.at[1])
    for copy in halo_copies(1, w_1):
        copy.start()
    prepare(1, w_1, w_2)
    inverse, moment = measures(gather("whole", slots_whole, send_1.at[1], recv_1.at[1]))
    set_stat(0, moment)

    normalize(w_1, u_1, inverse)
    squares, products = step(
        1, u_0, w_1, w_2, inverse,
        lambda d, high: linear[d * 8 : (d + 1) * 8, high * 128 : (high + 1) * 128],
    )
    scalars_start(2, "column", squares, products)
    for copy in halo_copies(2, w_2):
        copy.start()
    exchange_out_start(1, w_2, r_2)
    prepare(2, w_2, w_3)
    scalars_middle(2, "column", "layer")
    inverse, moment = scalars_end(2, "layer")
    set_stat(1, moment)
    set_stat(3, inverse)

    normalize(w_2, None, inverse)
    squares, products = step(
        2, u_1, w_2, w_3, inverse,
        lambda d, high: linear[d * 8 : (d + 1) * 8, high * 128 : (high + 1) * 128],
    )
    scalars_start(3, "column", squares, products)
    exchange_out_start(2, w_3, r_3)
    scalars_middle(3, "column", "layer")
    exchange_out_wait(1, w_2, r_2)
    inverse, moment = scalars_end(3, "layer")
    set_stat(2, moment)
    set_stat(4, inverse)
    exchange_out_wait(2, w_3, r_3)

    for e in range(3):
        wait_send(t.at[pl.ds(0, 63 * 16), :], send_sem.at[e], recv_sem.at[e])
    wait_send(slots_whole.at[pl.ds(0, 255)], send_1.at[1], recv_1.at[1])
    for r, group, group_2 in (
        (0, "plane", "line"),
        (2, "column", "layer"),
        (3, "column", "layer"),
    ):
        count, count_2 = groups[group][1], groups[group_2][1]
        wait_send(slots_1.at[r, pl.ds(0, count - 1)], send_1.at[r], recv_1.at[r])
        wait_send(slots_2.at[r, pl.ds(0, count_2 - 1)], send_2.at[r], recv_2.at[r])
    for k, w in enumerate((r_in, w_1, w_2)):
        for copy in halo_copies(k, w):
            copy.wait_send()


def finish_kernel(r_3, r_2, stats, last, prev, moments, v_3, v_2, out_3, out_2, held, kept, sem, store_sem):
    load = pltpu.make_async_copy(stats, held, sem.at[0])
    load_2 = pltpu.make_async_copy(r_2, v_2, sem.at[1])
    load_3 = pltpu.make_async_copy(r_3, v_3, sem.at[2])
    load.start()
    load_2.start()
    load_3.start()

    def finish(r, scale, out, stores):
        for high in range(8):
            block = jnp.concatenate(
                [r[pl.ds(high, 64, stride=16), :], r[pl.ds(8 + high, 64, stride=16), :]], axis=0
            )
            out[high * 128 : (high + 1) * 128, :] = block.T * scale
            stores[high].start()

    def stores_of(out, result, k):
        return [
            pltpu.make_async_copy(
                out.at[pl.ds(high * 128, 128), :], result.at[pl.ds(high * 128, 128), :], store_sem.at[k, high]
            )
            for high in range(8)
        ]

    store = pltpu.make_async_copy(kept, moments, sem.at[3])
    stores_2 = stores_of(out_2, prev, 0)
    stores_3 = stores_of(out_3, last, 1)
    load.wait()
    for k in range(STEPS):
        kept[k] = held[k]
    store.start()
    load_2.wait()
    finish(v_2, held[3], out_2, stores_2)
    load_3.wait()
    finish(v_3, held[4], out_3, stores_3)
    store.wait()
    for copy in stores_2 + stores_3:
        copy.wait()


def shards(state, operators, op_mask, site_bits, field, site_coupling, mode_coupling):
    block = jax.ShapeDtypeStruct((ROWS, LANES), F32)
    flat = pltpu.VMEM((ROWS, LANES), F32)
    cube = pltpu.VMEM((16, 64, LANES), F32)
    wide = pltpu.VMEM((LANES, ROWS), F32)
    dma = pltpu.SemaphoreType.DMA
    hbm = pl.BlockSpec(memory_space=pltpu.HBM)
    scalar = pl.BlockSpec(memory_space=pltpu.SMEM)
    carried = pl.pallas_call(
        kernel,
        out_shape=(block, block, jax.ShapeDtypeStruct((8,), F32)),
        in_specs=[hbm] * 7,
        out_specs=(hbm, hbm, scalar),
        scratch_shapes=[
            pltpu.SMEM((4, 8, 8), jnp.int32),
            pltpu.SMEM((4,), jnp.int32),
            pltpu.SMEM((4,), F32),
            pltpu.SMEM((14,), F32),
            pltpu.SMEM((64,), F32),
            flat,
            pltpu.VMEM((4, ROWS, ROWS), BF16),
            pltpu.VMEM((4, ROWS, ROWS), BF16),
            flat,
            cube,
            cube,
            cube,
            cube,
            wide,
            wide,
            pltpu.VMEM((LANES, ROWS), BF16),
            wide,
            wide,
            pltpu.VMEM((8, ROWS), F32),
            pltpu.VMEM((3, 2, 16, 8, LANES), F32),
            pltpu.VMEM((4, 64, 1, LANES), F32),
            pltpu.VMEM((4, 16, 1, LANES), F32),
            pltpu.VMEM((256, 1, LANES), F32),
            pltpu.VMEM((4, 1, LANES), F32),
            pltpu.VMEM((4, 1, LANES), F32),
            dma((7,)),
            dma((3,)),
            dma((2,)),
            dma((3,)),
            dma((3,)),
            dma((3, 2)),
            dma((3, 2)),
            dma((4,)),
            dma((4,)),
            dma((4,)),
            dma((4,)),
        ],
        compiler_params=pltpu.CompilerParams(
            collective_id=0, has_side_effects=True, vmem_limit_bytes=67043328
        ),
    )(state, operators, op_mask, site_bits, field, site_coupling, mode_coupling)
    return pl.pallas_call(
        finish_kernel,
        out_shape=(block, block, jax.ShapeDtypeStruct((STEPS,), F32)),
        in_specs=[hbm] * 3,
        out_specs=(hbm, hbm, hbm),
        scratch_shapes=[flat] * 4
        + [pltpu.SMEM((8,), F32), pltpu.SMEM((STEPS,), F32), dma((4,)), dma((2, 8))],
        compiler_params=pltpu.CompilerParams(vmem_limit_bytes=67043328),
    )(*carried)


def solution(mesh):
    in_specs = (P("site", "phonon"), P(), P(), P(), P(), P(), P())
    out_specs = (P("site", "phonon"), P("site", "phonon"), P())
    return jax.shard_map(shards, mesh=mesh, in_specs=in_specs, out_specs=out_specs, check_vma=False)
```

```python
import functools
import jax
import jax.numpy as jnp
from jax import lax
from jax.experimental import pallas as pl
from jax.experimental.pallas import tpu as pltpu
from jax.sharding import PartitionSpec as P

MESH = pl.DeviceIdType.MESH
F32 = jnp.float32
BF16 = jnp.bfloat16
ROWS = 1024
LANES = 128
STEPS = 3
EPSILON = 1e-06
ENTRIES = 33554432.0


def flipped(value, bit):
    size = 8 << bit
    parts = [value[i * size : (i + 1) * size] for i in range(LANES // size)]
    swapped = []
    for i in range(0, len(parts), 2):
        swapped += [parts[i + 1], parts[i]]
    return jnp.concatenate(swapped, axis=0)


def ring(offset, size):
    return min(offset % size, -offset % size)


def offsets(zs=1, xs=1, ys=1, cores=1):
    found = [
        (dz, dx, dy, dc)
        for dz in range(zs)
        for dx in range(xs)
        for dy in range(ys)
        for dc in range(cores)
        if (dz, dx, dy, dc) != (0, 0, 0, 0)
    ]
    return sorted(found, key=lambda o: -ring(o[0], 8) - ring(o[1], 4) - ring(o[2], 4))


PLANE = offsets(zs=8, xs=4, cores=2)
LINE = offsets(ys=4)
COLUMN = offsets(zs=8, cores=2)
LAYER = offsets(xs=4, ys=4)
ROW = offsets(xs=4)
WHOLE = offsets(zs=8, xs=4, ys=4, cores=2)


def finished(r, high):
    lower = r[pl.ds(high, 64, stride=16), :]
    upper = r[pl.ds(8 + high, 64, stride=16), :]
    return jnp.concatenate([lower, upper], axis=0).T


def kernel(
    state, ops, mask_in, site_bits_in, field_in, site_coupling_in, mode_coupling_in,
    r_3, ready, stats,
    mask, site_bits, field, site_coupling, mode_coupling,
    st, opv, a, t, r_in, r_2, out_2, w_1, w_2, w_3, u_0, u_1, ub, acc, linear, occ, halo,
    slots_1, slots_2, slots_whole, rows_1, rows_2,
    load_sem, self_sem, in_sem, line_sem, out_sem, send_sem, recv_sem, hsend_sem, hrecv_sem,
    send_1, recv_1, send_2, recv_2,
):
    site = lax.axis_index("site")
    phonon = lax.axis_index("phonon")
    z_lo, x = site // 4, site % 4
    y, q = phonon // 4, phonon % 4
    z_hi, core = q // 2, q % 2
    z = z_hi * 4 + z_lo
    mode = site * 4 + q

    def place_of(offset):
        dz, dx, dy, dc = offset
        z_at, x_at, y_at, core_at = (z + dz) % 8, (x + dx) % 4, (y + dy) % 4, (core + dc) % 2
        return (z_at % 4) * 4 + x_at, y_at, (z_at // 4) * 2 + core_at

    def device_of(offset):
        site_at, y_at, q_at = place_of(offset)
        return (site_at, y_at * 4 + q_at)

    barrier = pltpu.get_barrier_semaphore()
    for offset in PLANE + LINE:
        pl.semaphore_signal(barrier, inc=1, device_id=device_of(offset), device_id_type=MESH)

    load_state = pltpu.make_async_copy(state, st, load_sem.at[0])
    load_state.start()
    load_ops = pltpu.make_async_copy(ops, opv, load_sem.at[1])
    small = [
        pltpu.make_async_copy(source, target, load_sem.at[2 + i])
        for i, (source, target) in enumerate(
            (
                (mask_in, mask),
                (site_bits_in, site_bits),
                (field_in, field),
                (site_coupling_in, site_coupling),
                (mode_coupling_in, mode_coupling),
            )
        )
    ]
    for copy in small:
        copy.start()
    load_ops.start()

    load_state.wait()
    zero = jnp.zeros((8, LANES), F32)
    squares = zero
    for high in range(8):
        block = st[high * 128 : (high + 1) * 128, :]
        squares = squares + jnp.sum((block * block).reshape(16, 8, LANES), axis=0)
        turned = block.T
        t[pl.ds(high, 64, stride=16), :] = turned[:64]
        t[pl.ds(8 + high, 64, stride=16), :] = turned[64:]

    lane = lax.broadcasted_iota(jnp.int32, (1, LANES), 1)

    def fold(value):
        row = jnp.sum(value, axis=0, keepdims=True)
        return row + pltpu.roll(row, 64, 1)

    def wait_recv(ref, send, recv):
        pltpu.make_async_remote_copy(
            src_ref=ref, dst_ref=ref, send_sem=send, recv_sem=recv,
            device_id=(site, phonon), device_id_type=MESH,
        ).wait_recv()

    def wait_send(ref, send, recv):
        pltpu.make_async_remote_copy(
            src_ref=ref, dst_ref=ref, send_sem=send, recv_sem=recv,
            device_id=(site, phonon), device_id_type=MESH,
        ).wait_send()

    groups = {
        "line": (LINE, 4, y),
        "row": (ROW, 4, x),
        "column": (COLUMN, 16, z * 2 + core),
        "layer": (LAYER, 16, x * 4 + y),
        "whole": (WHOLE, 256, site * 16 + phonon),
    }

    def spread(group, src, slots, row, send, recv):
        members, count, index = groups[group]
        src[...] = row
        slots[index] = row
        for offset in members:
            pltpu.make_async_remote_copy(
                src_ref=src, dst_ref=slots.at[index], send_sem=send, recv_sem=recv,
                device_id=device_of(offset), device_id_type=MESH,
            ).start()

    def gather(group, slots, send, recv):
        members, count, index = groups[group]
        wait_recv(slots.at[pl.ds(0, count - 1)], send, recv)
        if count <= 16:
            return jnp.sum(slots[0:count], axis=0)
        value = slots[0:8]
        for i in range(8, count, 8):
            value = value + slots[i : i + 8]
        return jnp.sum(value, axis=0)

    def scalars_start(r, group, squares, products):
        row = jnp.where(lane < 64, fold(squares), fold(products))
        spread(group, rows_1.at[r], slots_1.at[r], row, send_1.at[r], recv_1.at[r])

    def scalars_middle(r, group, group_2):
        row = gather(group, slots_1.at[r], send_1.at[r], recv_1.at[r])
        spread(group_2, rows_2.at[r], slots_2.at[r], row, send_2.at[r], recv_2.at[r])

    def scalars_end(r, group_2):
        return measures(gather(group_2, slots_2.at[r], send_2.at[r], recv_2.at[r]))

    def measures(row):
        total = jnp.sum(jnp.where(lane < 64, row, 0.0), axis=1, keepdims=True)
        product = jnp.sum(jnp.where(lane < 64, 0.0, row), axis=1, keepdims=True)
        inverse = 1.0 / jnp.sqrt(total / ENTRIES + EPSILON)
        return inverse, product * inverse / ENTRIES

    def chunk2(ref, i):
        return ref.at[pl.ds(pl.multiple_of(i * 16, 16), 16), :]

    def chunk3(ref, site_at, q_at):
        return ref.at[site_at, pl.ds(pl.multiple_of(q_at * 16, 16), 16), :]

    early = (q == 0) | (q == 3)
    kind = jnp.where(early, 0, 1)

    def exchange_in_start():
        pltpu.make_async_copy(chunk2(t, mode), chunk3(r_in, site, q), in_sem.at[kind]).start()
        for offset in PLANE:
            site_at, y_at, q_at = place_of(offset)
            pltpu.make_async_remote_copy(
                src_ref=chunk2(t, site_at * 4 + q_at), dst_ref=chunk3(r_in, site, q),
                send_sem=send_sem.at[0], recv_sem=in_sem.at[kind],
                device_id=(site_at, y_at * 4 + q_at), device_id_type=MESH,
            ).start()

    def exchange_in_wait(which):
        wait_recv(t.at[pl.ds(0, 32 * 16), :], send_sem.at[0], in_sem.at[which])

    def exchange_out_self(e, w, r):
        return pltpu.make_async_copy(chunk3(w, site, q), chunk2(r, mode), self_sem.at[e])

    def exchange_out_start(e, w, r):
        exchange_out_self(e, w, r).start()
        for offset in PLANE:
            site_at, y_at, q_at = place_of(offset)
            pltpu.make_async_remote_copy(
                src_ref=chunk3(w, site_at, q_at), dst_ref=chunk2(r, mode),
                send_sem=send_sem.at[e], recv_sem=recv_sem.at[e],
                device_id=(site_at, y_at * 4 + q_at), device_id_type=MESH,
            ).start()

    def exchange_out_wait(e, w, r):
        exchange_out_self(e, w, r).wait()
        wait_recv(t.at[pl.ds(0, 63 * 16), :], send_sem.at[e], recv_sem.at[e])

    def halo_copies(k, w):
        up = pltpu.make_async_remote_copy(
            src_ref=w.at[:, pl.ds(56, 8), :], dst_ref=halo.at[k, 0],
            send_sem=hsend_sem.at[k, 0], recv_sem=hrecv_sem.at[k, 0],
            device_id=(site, ((y + 1) % 4) * 4 + q), device_id_type=MESH,
        )
        down = pltpu.make_async_remote_copy(
            src_ref=w.at[:, pl.ds(0, 8), :], dst_ref=halo.at[k, 1],
            send_sem=hsend_sem.at[k, 1], recv_sem=hrecv_sem.at[k, 1],
            device_id=(site, ((y + 3) % 4) * 4 + q), device_id_type=MESH,
        )
        return up, down

    pl.semaphore_wait(barrier, 66)
    scalars_start(0, "column", squares, zero)
    pl.when(early)(exchange_in_start)

    for copy in small:
        copy.wait()
    chosen = [site_bits[b] for b in range(4)]
    fields = [field[c] for c in chosen]
    device_coupling = [site_coupling[c] for c in chosen]

    place = lax.broadcasted_iota(jnp.int32, (8, ROWS), 1)
    weights = jnp.zeros((8, ROWS), F32)
    for j in range(10):
        weights = weights + site_coupling[4 + j] * ((place >> j) & 1).astype(F32)
    occ[...] = weights

    level = lax.broadcasted_iota(jnp.int32, (8, LANES), 0) + y * 8
    mode_weight = mode_coupling[mode] / jnp.sqrt(F32(32.0))
    lower_weight = mode_weight * jnp.sqrt(level.astype(F32))
    upper_weight = mode_weight * jnp.where(level < 31, jnp.sqrt((level + 1).astype(F32)), 0.0)

    load_ops.wait()

    def mask_operator(b):
        @pl.loop(0, 8)
        def _(i):
            rows = pl.ds(pl.multiple_of(i * 128, 128), 128)
            for j in range(8):
                keep = mask[chosen[b], i, j] > 0
                tile = opv[chosen[b], rows, j * 128 : (j + 1) * 128]
                a[b, j * 128 : (j + 1) * 128, rows] = jnp.where(keep, tile, jnp.zeros_like(tile)).T

    for b in range(4):
        mask_operator(b)
    pl.when(jnp.logical_not(early))(exchange_in_start)
    scalars_middle(0, "column", "row")
    row = gather("row", slots_2.at[0], send_2.at[0], recv_2.at[0])
    spread("line", rows_1.at[1], slots_1.at[1], row, line_sem.at[0], line_sem.at[1])
    exchange_in_wait(0)
    for copy in halo_copies(0, r_in):
        copy.start()
    exchange_in_wait(1)
    inverse, _ = measures(gather("line", slots_1.at[1], line_sem.at[0], line_sem.at[1]))

    sublane = lax.broadcasted_iota(jnp.int32, (8, LANES), 0)

    def normalize(w, u, inverse):
        scale = jnp.broadcast_to(inverse, (8, LANES))

        @pl.loop(0, 8)
        def _(e):
            for high in range(8):
                cols = slice(high * 128, (high + 1) * 128)
                first = w[2 * e, pl.ds(high, 8, stride=8), :] * scale
                second = w[2 * e + 1, pl.ds(high, 8, stride=8), :] * scale
                both = jnp.concatenate([first, second], axis=0)
                rows = pl.ds(pl.multiple_of(e * 16, 16), 16)
                if u is not None:
                    u[rows, cols] = both
                ub[rows, cols] = both.astype(BF16)

    def bits_of(d):
        if isinstance(d, int):
            return [jnp.int32((d >> b) & 1) for b in range(4)]
        return [(d // (1 << b)) % 2 for b in range(4)]

    def ladder_of(k, d, high, here):
        cols = slice(high * 128, (high + 1) * 128)
        constant = F32(0.0)
        for b, bit in enumerate(bits_of(d)):
            constant = constant + device_coupling[b] * bit.astype(F32)
        below = jnp.broadcast_to(halo[k, 0, d, high : high + 1, :], (8, LANES))
        above = jnp.broadcast_to(halo[k, 1, d, high : high + 1, :], (8, LANES))
        lower = jnp.where(sublane == 0, below, pltpu.roll(here, 1, 0))
        upper = jnp.where(sublane == 7, above, pltpu.roll(here, 7, 0))
        return (occ[:, cols] + constant) * (lower_weight * lower + upper_weight * upper)

    def prepare(k, w_before, w):
        for copy in halo_copies(k, w):
            copy.wait_recv()

        @pl.loop(0, 16)
        def _(d):
            bits = bits_of(d)
            rows = pl.ds(pl.multiple_of(d * 8, 8), 8)
            for high in range(8):
                cols = slice(high * 128, (high + 1) * 128)
                here = w_before[d, pl.ds(high, 8, stride=8), :]
                value = ladder_of(k, d, high, here)
                for b in range(4):
                    other = d + (1 - 2 * bits[b]) * (1 << b)
                    value = value + fields[b] * w_before[other, pl.ds(high, 8, stride=8), :]
                linear[rows, cols] = value

    def linear_part(w_before, k, d, high):
        value = ladder_of(k, d, high, w_before[d, pl.ds(high, 8, stride=8), :])
        for b in range(4):
            value = value + fields[b] * w_before[d ^ (1 << b), pl.ds(high, 8, stride=8), :]
        return value

    def step(k, u_before, w_before, w, inverse, part):
        scale = jnp.broadcast_to(inverse, (8, LANES))
        total = None
        for b in range(4):
            product = flipped(jnp.dot(ub[...], a[b], preferred_element_type=F32), b)
            total = product if total is None else total + product
        squares, products = zero, zero
        for d in range(16):
            rows = slice(d * 8, (d + 1) * 8)
            for high in range(8):
                cols = slice(high * 128, (high + 1) * 128)
                new = total[rows, cols] + part(d, high) * scale
                if k > 0:
                    new = 2.0 * new - u_before[rows, cols] * scale
                w[d, pl.ds(high, 8, stride=8), :] = new
                squares = squares + new * new
                products = products + u_0[rows, cols] * new
        return squares, products

    def multiply():
        total = None
        for b in range(4):
            product = flipped(jnp.dot(ub[...], a[b], preferred_element_type=F32), b)
            total = product if total is None else total + product
        acc[...] = total

    def combine(k, u_before, w, inverse, send=None):
        scale = jnp.broadcast_to(inverse, (8, LANES))

        def body(i, carry):
            squares, products = carry
            d = (site + 1 + i) % 16
            rows = pl.ds(pl.multiple_of(d * 8, 8), 8)
            for high in range(8):
                cols = slice(high * 128, (high + 1) * 128)
                new = acc[rows, cols] + linear[rows, cols] * scale
                if k > 0:
                    new = 2.0 * new - u_before[rows, cols] * scale
                w[d, pl.ds(high, 8, stride=8), :] = new
                squares = squares + new * new
                products = products + u_0[rows, cols] * new
            if send is not None:
                send(i)
            return squares, products

        return lax.fori_loop(0, 16, body, (zero, zero))

    def set_stat(k, value):
        stats[k] = value[0, 0]

    normalize(r_in, u_0, inverse)
    for copy in halo_copies(0, r_in):
        copy.wait_recv()
    squares, products = step(
        0, None, r_in, w_1, inverse, lambda d, high: linear_part(r_in, 0, d, high)
    )
    row = jnp.where(lane < 64, fold(squares), fold(products))
    spread("whole", rows_2.at[1], slots_whole, row, send_1.at[1], recv_1.at[1])
    for copy in halo_copies(1, w_1):
        copy.start()
    prepare(1, w_1, w_2)
    inverse, moment = measures(gather("whole", slots_whole, send_1.at[1], recv_1.at[1]))
    set_stat(0, moment)

    normalize(w_1, u_1, inverse)
    squares, products = step(
        1, u_0, w_1, w_2, inverse,
        lambda d, high: linear[d * 8 : (d + 1) * 8, high * 128 : (high + 1) * 128],
    )
    scalars_start(2, "column", squares, products)
    for copy in halo_copies(2, w_2):
        copy.start()
    exchange_out_start(1, w_2, r_2)
    prepare(2, w_2, w_3)
    scalars_middle(2, "column", "layer")
    inverse, moment = scalars_end(2, "layer")
    set_stat(1, moment)
    inverse_2 = inverse

    normalize(w_2, None, inverse)
    squares, products = step(
        2, u_1, w_2, w_3, inverse,
        lambda d, high: linear[d * 8 : (d + 1) * 8, high * 128 : (high + 1) * 128],
    )
    scalars_start(3, "column", squares, products)
    exchange_out_start(2, w_3, r_3)
    scalars_middle(3, "column", "layer")
    exchange_out_wait(1, w_2, r_2)
    scale_2 = jnp.broadcast_to(inverse_2, (128, LANES))
    for high in range(8):
        out_2[high * 128 : (high + 1) * 128, :] = finished(r_2, high) * scale_2
    store_2 = pltpu.make_async_copy(out_2, ready, out_sem)
    store_2.start()
    inverse, moment = scalars_end(3, "layer")
    set_stat(2, moment)
    set_stat(3, inverse)
    exchange_out_wait(2, w_3, r_3)
    store_2.wait()

    for e in range(3):
        wait_send(t.at[pl.ds(0, 63 * 16), :], send_sem.at[e], recv_sem.at[e])
    wait_send(slots_1.at[1, pl.ds(0, 3)], line_sem.at[0], line_sem.at[1])
    wait_send(slots_whole.at[pl.ds(0, 255)], send_1.at[1], recv_1.at[1])
    for r, group, group_2 in (
        (0, "column", "row"),
        (2, "column", "layer"),
        (3, "column", "layer"),
    ):
        count, count_2 = groups[group][1], groups[group_2][1]
        wait_send(slots_1.at[r, pl.ds(0, count - 1)], send_1.at[r], recv_1.at[r])
        wait_send(slots_2.at[r, pl.ds(0, count_2 - 1)], send_2.at[r], recv_2.at[r])
    for k, w in enumerate((r_in, w_1, w_2)):
        for copy in halo_copies(k, w):
            copy.wait_send()


def finish_kernel(r_3, ready, stats, last, prev, moments, v_3, v_2, out_3, held, kept, sem, store_sem):
    load = pltpu.make_async_copy(stats, held, sem.at[0])
    load_3 = pltpu.make_async_copy(r_3, v_3, sem.at[1])
    load_2 = pltpu.make_async_copy(ready, v_2, sem.at[2])
    store = pltpu.make_async_copy(kept, moments, sem.at[3])
    store_2 = pltpu.make_async_copy(v_2, prev, sem.at[4])
    load.start()
    load_3.start()
    load_2.start()
    load.wait()
    for k in range(STEPS):
        kept[k] = held[k]
    store.start()
    load_3.wait()
    scale = held[3]
    stores = []
    for high in range(8):
        rows = pl.ds(high * 128, 128)
        out_3[rows, :] = finished(v_3, high) * scale
        stores.append(pltpu.make_async_copy(out_3.at[rows, :], last.at[rows, :], store_sem.at[high]))
        stores[high].start()
        if high == 0:
            load_2.wait()
            store_2.start()
    for copy in stores + [store, store_2]:
        copy.wait()


def shards(state, operators, op_mask, site_bits, field, site_coupling, mode_coupling):
    block = jax.ShapeDtypeStruct((ROWS, LANES), F32)
    flat = pltpu.VMEM((ROWS, LANES), F32)
    cube = pltpu.VMEM((16, 64, LANES), F32)
    wide = pltpu.VMEM((LANES, ROWS), F32)
    dma = pltpu.SemaphoreType.DMA
    hbm = pl.BlockSpec(memory_space=pltpu.HBM)
    scalar = pl.BlockSpec(memory_space=pltpu.SMEM)
    carried = pl.pallas_call(
        kernel,
        out_shape=(block, block, jax.ShapeDtypeStruct((8,), F32)),
        in_specs=[hbm] * 7,
        out_specs=(hbm, hbm, scalar),
        scratch_shapes=[
            pltpu.SMEM((4, 8, 8), jnp.int32),
            pltpu.SMEM((4,), jnp.int32),
            pltpu.SMEM((4,), F32),
            pltpu.SMEM((14,), F32),
            pltpu.SMEM((64,), F32),
            flat,
            pltpu.VMEM((4, ROWS, ROWS), BF16),
            pltpu.VMEM((4, ROWS, ROWS), BF16),
            flat,
            cube,
            flat,
            flat,
            cube,
            cube,
            cube,
            wide,
            wide,
            pltpu.VMEM((LANES, ROWS), BF16),
            wide,
            wide,
            pltpu.VMEM((8, ROWS), F32),
            pltpu.VMEM((3, 2, 16, 8, LANES), F32),
            pltpu.VMEM((4, 16, 1, LANES), F32),
            pltpu.VMEM((4, 16, 1, LANES), F32),
            pltpu.VMEM((256, 1, LANES), F32),
            pltpu.VMEM((4, 1, LANES), F32),
            pltpu.VMEM((4, 1, LANES), F32),
            dma((7,)),
            dma((3,)),
            dma((2,)),
            dma((2,)),
            dma,
            dma((3,)),
            dma((3,)),
            dma((3, 2)),
            dma((3, 2)),
            dma((4,)),
            dma((4,)),
            dma((4,)),
            dma((4,)),
        ],
        compiler_params=pltpu.CompilerParams(
            collective_id=0, has_side_effects=True, vmem_limit_bytes=67043328
        ),
    )(state, operators, op_mask, site_bits, field, site_coupling, mode_coupling)
    return pl.pallas_call(
        finish_kernel,
        out_shape=(block, block, jax.ShapeDtypeStruct((STEPS,), F32)),
        in_specs=[hbm] * 3,
        out_specs=(hbm, hbm, hbm),
        scratch_shapes=[flat] * 3
        + [pltpu.SMEM((8,), F32), pltpu.SMEM((STEPS,), F32), dma((5,)), dma((8,))],
        compiler_params=pltpu.CompilerParams(vmem_limit_bytes=67043328),
    )(*carried)


def solution(mesh):
    in_specs = (P("site", "phonon"), P(), P(), P(), P(), P(), P())
    out_specs = (P("site", "phonon"), P("site", "phonon"), P())
    return jax.shard_map(shards, mesh=mesh, in_specs=in_specs, out_specs=out_specs, check_vma=False)
```

```python
import functools
import jax
import jax.numpy as jnp
from jax import lax
from jax.experimental import pallas as pl
from jax.experimental.pallas import tpu as pltpu
from jax.sharding import PartitionSpec as P

MESH = pl.DeviceIdType.MESH
F32 = jnp.float32
BF16 = jnp.bfloat16
ROWS = 1024
LANES = 128
STEPS = 3
EPSILON = 1e-06
ENTRIES = 33554432.0


def flipped(value, bit):
    size = 8 << bit
    parts = [value[i * size : (i + 1) * size] for i in range(LANES // size)]
    swapped = []
    for i in range(0, len(parts), 2):
        swapped += [parts[i + 1], parts[i]]
    return jnp.concatenate(swapped, axis=0)


def ring(offset, size):
    return min(offset % size, -offset % size)


def offsets(zs=1, xs=1, ys=1, cores=1):
    found = [
        (dz, dx, dy, dc)
        for dz in range(zs)
        for dx in range(xs)
        for dy in range(ys)
        for dc in range(cores)
        if (dz, dx, dy, dc) != (0, 0, 0, 0)
    ]
    return sorted(found, key=lambda o: -ring(o[0], 8) - ring(o[1], 4) - ring(o[2], 4))


PLANE = offsets(zs=8, xs=4, cores=2)
LINE = offsets(ys=4)
COLUMN = offsets(zs=8, cores=2)
LAYER = offsets(xs=4, ys=4)
ROW = offsets(xs=4)
WHOLE = offsets(zs=8, xs=4, ys=4, cores=2)


def finished(r, high):
    lower = r[pl.ds(high, 64, stride=16), :]
    upper = r[pl.ds(8 + high, 64, stride=16), :]
    return jnp.concatenate([lower, upper], axis=0).T


def kernel(
    state, ops, mask_in, site_bits_in, field_in, site_coupling_in, mode_coupling_in,
    r_3, ready, stats,
    mask, site_bits, field, site_coupling, mode_coupling,
    st, opv, a, t, r_in, r_2, out_2, w_1, w_2, w_3, u_0, u_1, ub, acc, linear, occ, halo,
    slots_1, slots_2, slots_whole, rows_1, rows_2,
    load_sem, self_sem, in_sem, line_sem, out_sem, send_sem, recv_sem, hsend_sem, hrecv_sem,
    send_1, recv_1, send_2, recv_2,
):
    site = lax.axis_index("site")
    phonon = lax.axis_index("phonon")
    z_lo, x = site // 4, site % 4
    y, q = phonon // 4, phonon % 4
    z_hi, core = q // 2, q % 2
    z = z_hi * 4 + z_lo
    mode = site * 4 + q

    def place_of(offset):
        dz, dx, dy, dc = offset
        z_at, x_at, y_at, core_at = (z + dz) % 8, (x + dx) % 4, (y + dy) % 4, (core + dc) % 2
        return (z_at % 4) * 4 + x_at, y_at, (z_at // 4) * 2 + core_at

    def device_of(offset):
        site_at, y_at, q_at = place_of(offset)
        return (site_at, y_at * 4 + q_at)

    barrier = pltpu.get_barrier_semaphore()
    for offset in PLANE + LINE:
        pl.semaphore_signal(barrier, inc=1, device_id=device_of(offset), device_id_type=MESH)

    load_state = pltpu.make_async_copy(state, st, load_sem.at[0])
    load_state.start()
    load_ops = pltpu.make_async_copy(ops, opv, load_sem.at[1])
    small = [
        pltpu.make_async_copy(source, target, load_sem.at[2 + i])
        for i, (source, target) in enumerate(
            (
                (mask_in, mask),
                (site_bits_in, site_bits),
                (field_in, field),
                (site_coupling_in, site_coupling),
                (mode_coupling_in, mode_coupling),
            )
        )
    ]
    for copy in small:
        copy.start()
    load_ops.start()

    load_state.wait()
    zero = jnp.zeros((8, LANES), F32)
    squares = zero
    for high in range(8):
        block = st[high * 128 : (high + 1) * 128, :]
        squares = squares + jnp.sum((block * block).reshape(16, 8, LANES), axis=0)
        turned = block.T
        t[pl.ds(high, 64, stride=16), :] = turned[:64]
        t[pl.ds(8 + high, 64, stride=16), :] = turned[64:]

    lane = lax.broadcasted_iota(jnp.int32, (1, LANES), 1)

    def fold(value):
        row = jnp.sum(value, axis=0, keepdims=True)
        return row + pltpu.roll(row, 64, 1)

    def wait_recv(ref, send, recv):
        pltpu.make_async_remote_copy(
            src_ref=ref, dst_ref=ref, send_sem=send, recv_sem=recv,
            device_id=(site, phonon), device_id_type=MESH,
        ).wait_recv()

    def wait_send(ref, send, recv):
        pltpu.make_async_remote_copy(
            src_ref=ref, dst_ref=ref, send_sem=send, recv_sem=recv,
            device_id=(site, phonon), device_id_type=MESH,
        ).wait_send()

    groups = {
        "line": (LINE, 4, y),
        "row": (ROW, 4, x),
        "column": (COLUMN, 16, z * 2 + core),
        "layer": (LAYER, 16, x * 4 + y),
        "whole": (WHOLE, 256, site * 16 + phonon),
    }

    def spread(group, src, slots, row, send, recv):
        members, count, index = groups[group]
        src[...] = row
        slots[index] = row
        for offset in members:
            pltpu.make_async_remote_copy(
                src_ref=src, dst_ref=slots.at[index], send_sem=send, recv_sem=recv,
                device_id=device_of(offset), device_id_type=MESH,
            ).start()

    def gather(group, slots, send, recv):
        members, count, index = groups[group]
        wait_recv(slots.at[pl.ds(0, count - 1)], send, recv)
        if count <= 16:
            return jnp.sum(slots[0:count], axis=0)
        value = slots[0:8]
        for i in range(8, count, 8):
            value = value + slots[i : i + 8]
        return jnp.sum(value, axis=0)

    def scalars_start(r, group, squares, products):
        row = jnp.where(lane < 64, fold(squares), fold(products))
        spread(group, rows_1.at[r], slots_1.at[r], row, send_1.at[r], recv_1.at[r])

    def scalars_middle(r, group, group_2):
        row = gather(group, slots_1.at[r], send_1.at[r], recv_1.at[r])
        spread(group_2, rows_2.at[r], slots_2.at[r], row, send_2.at[r], recv_2.at[r])

    def scalars_end(r, group_2):
        return measures(gather(group_2, slots_2.at[r], send_2.at[r], recv_2.at[r]))

    def measures(row):
        total = jnp.sum(jnp.where(lane < 64, row, 0.0), axis=1, keepdims=True)
        product = jnp.sum(jnp.where(lane < 64, 0.0, row), axis=1, keepdims=True)
        inverse = 1.0 / jnp.sqrt(total / ENTRIES + EPSILON)
        return inverse, product * inverse / ENTRIES

    def chunk2(ref, i):
        return ref.at[pl.ds(pl.multiple_of(i * 16, 16), 16), :]

    def chunk3(ref, site_at, q_at):
        return ref.at[site_at, pl.ds(pl.multiple_of(q_at * 16, 16), 16), :]

    early = (q == 0) | (q == 3)
    kind = jnp.where(early, 0, 1)

    def exchange_in_start():
        pltpu.make_async_copy(chunk2(t, mode), chunk3(r_in, site, q), in_sem.at[kind]).start()
        for offset in PLANE:
            site_at, y_at, q_at = place_of(offset)
            pltpu.make_async_remote_copy(
                src_ref=chunk2(t, site_at * 4 + q_at), dst_ref=chunk3(r_in, site, q),
                send_sem=send_sem.at[0], recv_sem=in_sem.at[kind],
                device_id=(site_at, y_at * 4 + q_at), device_id_type=MESH,
            ).start()

    def exchange_in_wait(which):
        wait_recv(t.at[pl.ds(0, 32 * 16), :], send_sem.at[0], in_sem.at[which])

    def exchange_out_self(e, w, r):
        return pltpu.make_async_copy(chunk3(w, site, q), chunk2(r, mode), self_sem.at[e])

    def exchange_out_start(e, w, r):
        exchange_out_self(e, w, r).start()
        for offset in PLANE:
            site_at, y_at, q_at = place_of(offset)
            pltpu.make_async_remote_copy(
                src_ref=chunk3(w, site_at, q_at), dst_ref=chunk2(r, mode),
                send_sem=send_sem.at[e], recv_sem=recv_sem.at[e],
                device_id=(site_at, y_at * 4 + q_at), device_id_type=MESH,
            ).start()

    def exchange_out_wait(e, w, r):
        exchange_out_self(e, w, r).wait()
        wait_recv(t.at[pl.ds(0, 63 * 16), :], send_sem.at[e], recv_sem.at[e])

    def halo_copies(k, w):
        up = pltpu.make_async_remote_copy(
            src_ref=w.at[:, pl.ds(56, 8), :], dst_ref=halo.at[k, 0],
            send_sem=hsend_sem.at[k, 0], recv_sem=hrecv_sem.at[k, 0],
            device_id=(site, ((y + 1) % 4) * 4 + q), device_id_type=MESH,
        )
        down = pltpu.make_async_remote_copy(
            src_ref=w.at[:, pl.ds(0, 8), :], dst_ref=halo.at[k, 1],
            send_sem=hsend_sem.at[k, 1], recv_sem=hrecv_sem.at[k, 1],
            device_id=(site, ((y + 3) % 4) * 4 + q), device_id_type=MESH,
        )
        return up, down

    pl.semaphore_wait(barrier, 66)
    scalars_start(0, "column", squares, zero)
    pl.when(early)(exchange_in_start)

    for copy in small:
        copy.wait()
    chosen = [site_bits[b] for b in range(4)]
    fields = [field[c] for c in chosen]
    device_coupling = [site_coupling[c] for c in chosen]

    place = lax.broadcasted_iota(jnp.int32, (8, ROWS), 1)
    weights = jnp.zeros((8, ROWS), F32)
    for j in range(10):
        weights = weights + site_coupling[4 + j] * ((place >> j) & 1).astype(F32)
    occ[...] = weights

    level = lax.broadcasted_iota(jnp.int32, (8, LANES), 0) + y * 8
    mode_weight = mode_coupling[mode] / jnp.sqrt(F32(32.0))
    lower_weight = mode_weight * jnp.sqrt(level.astype(F32))
    upper_weight = mode_weight * jnp.where(level < 31, jnp.sqrt((level + 1).astype(F32)), 0.0)

    load_ops.wait()

    def mask_operator(b):
        @pl.loop(0, 8)
        def _(i):
            rows = pl.ds(pl.multiple_of(i * 128, 128), 128)
            for j in range(8):
                keep = mask[chosen[b], i, j] > 0
                tile = opv[chosen[b], rows, j * 128 : (j + 1) * 128]
                a[b, j * 128 : (j + 1) * 128, rows] = jnp.where(keep, tile, jnp.zeros_like(tile)).T

    for b in range(4):
        mask_operator(b)
    pl.when(jnp.logical_not(early))(exchange_in_start)
    scalars_middle(0, "column", "row")
    row = gather("row", slots_2.at[0], send_2.at[0], recv_2.at[0])
    spread("line", rows_1.at[1], slots_1.at[1], row, line_sem.at[0], line_sem.at[1])
    exchange_in_wait(0)
    for copy in halo_copies(0, r_in):
        copy.start()
    exchange_in_wait(1)
    inverse, _ = measures(gather("line", slots_1.at[1], line_sem.at[0], line_sem.at[1]))

    sublane = lax.broadcasted_iota(jnp.int32, (8, LANES), 0)

    def normalize(w, u, inverse):
        scale = jnp.broadcast_to(inverse, (8, LANES))

        @pl.loop(0, 8)
        def _(e):
            for high in range(8):
                cols = slice(high * 128, (high + 1) * 128)
                first = w[2 * e, pl.ds(high, 8, stride=8), :] * scale
                second = w[2 * e + 1, pl.ds(high, 8, stride=8), :] * scale
                both = jnp.concatenate([first, second], axis=0)
                rows = pl.ds(pl.multiple_of(e * 16, 16), 16)
                if u is not None:
                    u[rows, cols] = both
                ub[rows, cols] = both.astype(BF16)

    def bits_of(d):
        if isinstance(d, int):
            return [jnp.int32((d >> b) & 1) for b in range(4)]
        return [(d // (1 << b)) % 2 for b in range(4)]

    def occupancy(d, high):
        constant = F32(0.0)
        for b, bit in enumerate(bits_of(d)):
            constant = constant + device_coupling[b] * bit.astype(F32)
        return occ[:, high * 128 : (high + 1) * 128] + constant

    def halo_rows(k, d, high):
        below = jnp.broadcast_to(halo[k, 0, d, high : high + 1, :], (8, LANES))
        above = jnp.broadcast_to(halo[k, 1, d, high : high + 1, :], (8, LANES))
        return below, above

    def ladder_of(k, d, high, here):
        below, above = halo_rows(k, d, high)
        lower = jnp.where(sublane == 0, below, pltpu.roll(here, 1, 0))
        upper = jnp.where(sublane == 7, above, pltpu.roll(here, 7, 0))
        return occupancy(d, high) * (lower_weight * lower + upper_weight * upper)

    def prepare(k, w_before, w):
        for copy in halo_copies(k, w):
            copy.wait_recv()

        @pl.loop(0, 16)
        def _(d):
            bits = bits_of(d)
            rows = pl.ds(pl.multiple_of(d * 8, 8), 8)
            for high in range(8):
                cols = slice(high * 128, (high + 1) * 128)
                here = w_before[d, pl.ds(high, 8, stride=8), :]
                value = ladder_of(k, d, high, here)
                for b in range(4):
                    other = d + (1 - 2 * bits[b]) * (1 << b)
                    value = value + fields[b] * w_before[other, pl.ds(high, 8, stride=8), :]
                linear[rows, cols] = value

    def first_step(w, inverse):
        scale = jnp.broadcast_to(inverse, (8, LANES))
        total = None
        for b in range(4):
            product = flipped(jnp.dot(ub[...], a[b], preferred_element_type=F32), b)
            total = product if total is None else total + product
        inner_lower = jnp.where(sublane == 0, 0.0, lower_weight)
        inner_upper = jnp.where(sublane == 7, 0.0, upper_weight)
        for d in range(16):
            rows = slice(d * 8, (d + 1) * 8)
            for high in range(8):
                cols = slice(high * 128, (high + 1) * 128)
                here = r_in[d, pl.ds(high, 8, stride=8), :]
                value = occupancy(d, high) * (
                    inner_lower * pltpu.roll(here, 1, 0) + inner_upper * pltpu.roll(here, 7, 0)
                )
                for b in range(4):
                    value = value + fields[b] * r_in[d ^ (1 << b), pl.ds(high, 8, stride=8), :]
                acc[rows, cols] = total[rows, cols] + value * scale
        for copy in halo_copies(0, r_in):
            copy.wait_recv()
        outer_lower = jnp.where(sublane == 0, lower_weight, 0.0) * scale
        outer_upper = jnp.where(sublane == 7, upper_weight, 0.0) * scale
        squares, products = zero, zero
        for d in range(16):
            rows = slice(d * 8, (d + 1) * 8)
            for high in range(8):
                cols = slice(high * 128, (high + 1) * 128)
                below, above = halo_rows(0, d, high)
                new = acc[rows, cols] + occupancy(d, high) * (
                    outer_lower * below + outer_upper * above
                )
                w[d, pl.ds(high, 8, stride=8), :] = new
                squares = squares + new * new
                products = products + u_0[rows, cols] * new
        return squares, products

    def step(u_before, w, inverse, part):
        scale = jnp.broadcast_to(inverse, (8, LANES))
        total = None
        for b in range(4):
            product = flipped(jnp.dot(ub[...], a[b], preferred_element_type=F32), b)
            total = product if total is None else total + product
        squares, products = zero, zero
        for d in range(16):
            rows = slice(d * 8, (d + 1) * 8)
            for high in range(8):
                cols = slice(high * 128, (high + 1) * 128)
                new = total[rows, cols] + part(d, high) * scale
                new = 2.0 * new - u_before[rows, cols] * scale
                w[d, pl.ds(high, 8, stride=8), :] = new
                squares = squares + new * new
                products = products + u_0[rows, cols] * new
        return squares, products

    def set_stat(k, value):
        stats[k] = value[0, 0]

    normalize(r_in, u_0, inverse)
    squares, products = first_step(w_1, inverse)
    row = jnp.where(lane < 64, fold(squares), fold(products))
    spread("whole", rows_2.at[1], slots_whole, row, send_1.at[1], recv_1.at[1])
    for copy in halo_copies(1, w_1):
        copy.start()
    prepare(1, w_1, w_2)
    inverse, moment = measures(gather("whole", slots_whole, send_1.at[1], recv_1.at[1]))
    set_stat(0, moment)

    normalize(w_1, u_1, inverse)
    squares, products = step(
        u_0, w_2, inverse,
        lambda d, high: linear[d * 8 : (d + 1) * 8, high * 128 : (high + 1) * 128],
    )
    scalars_start(2, "column", squares, products)
    for copy in halo_copies(2, w_2):
        copy.start()
    exchange_out_start(1, w_2, r_2)
    prepare(2, w_2, w_3)
    scalars_middle(2, "column", "layer")
    inverse, moment = scalars_end(2, "layer")
    set_stat(1, moment)
    inverse_2 = inverse

    normalize(w_2, None, inverse)
    squares, products = step(
        u_1, w_3, inverse,
        lambda d, high: linear[d * 8 : (d + 1) * 8, high * 128 : (high + 1) * 128],
    )
    scalars_start(3, "column", squares, products)
    exchange_out_start(2, w_3, r_3)
    scalars_middle(3, "column", "layer")
    exchange_out_wait(1, w_2, r_2)
    scale_2 = jnp.broadcast_to(inverse_2, (128, LANES))
    for high in range(8):
        out_2[high * 128 : (high + 1) * 128, :] = finished(r_2, high) * scale_2
    store_2 = pltpu.make_async_copy(out_2, ready, out_sem)
    store_2.start()
    inverse, moment = scalars_end(3, "layer")
    set_stat(2, moment)
    set_stat(3, inverse)
    exchange_out_wait(2, w_3, r_3)
    store_2.wait()

    for e in range(3):
        wait_send(t.at[pl.ds(0, 63 * 16), :], send_sem.at[e], recv_sem.at[e])
    wait_send(slots_1.at[1, pl.ds(0, 3)], line_sem.at[0], line_sem.at[1])
    wait_send(slots_whole.at[pl.ds(0, 255)], send_1.at[1], recv_1.at[1])
    for r, group, group_2 in (
        (0, "column", "row"),
        (2, "column", "layer"),
        (3, "column", "layer"),
    ):
        count, count_2 = groups[group][1], groups[group_2][1]
        wait_send(slots_1.at[r, pl.ds(0, count - 1)], send_1.at[r], recv_1.at[r])
        wait_send(slots_2.at[r, pl.ds(0, count_2 - 1)], send_2.at[r], recv_2.at[r])
    for k, w in enumerate((r_in, w_1, w_2)):
        for copy in halo_copies(k, w):
            copy.wait_send()


def finish_kernel(r_3, ready, stats, last, prev, moments, v_3, v_2, out_3, held, kept, sem, store_sem):
    load = pltpu.make_async_copy(stats, held, sem.at[0])
    load_3 = pltpu.make_async_copy(r_3, v_3, sem.at[1])
    load_2 = pltpu.make_async_copy(ready, v_2, sem.at[2])
    store = pltpu.make_async_copy(kept, moments, sem.at[3])
    store_2 = pltpu.make_async_copy(v_2, prev, sem.at[4])
    load.start()
    load_3.start()
    load_2.start()
    load.wait()
    for k in range(STEPS):
        kept[k] = held[k]
    store.start()
    load_3.wait()
    scale = held[3]
    stores = []
    for high in range(8):
        rows = pl.ds(high * 128, 128)
        out_3[rows, :] = finished(v_3, high) * scale
        stores.append(pltpu.make_async_copy(out_3.at[rows, :], last.at[rows, :], store_sem.at[high]))
        stores[high].start()
        if high == 0:
            load_2.wait()
            store_2.start()
    for copy in stores + [store, store_2]:
        copy.wait()


def shards(state, operators, op_mask, site_bits, field, site_coupling, mode_coupling):
    block = jax.ShapeDtypeStruct((ROWS, LANES), F32)
    flat = pltpu.VMEM((ROWS, LANES), F32)
    cube = pltpu.VMEM((16, 64, LANES), F32)
    wide = pltpu.VMEM((LANES, ROWS), F32)
    dma = pltpu.SemaphoreType.DMA
    hbm = pl.BlockSpec(memory_space=pltpu.HBM)
    scalar = pl.BlockSpec(memory_space=pltpu.SMEM)
    carried = pl.pallas_call(
        kernel,
        out_shape=(block, block, jax.ShapeDtypeStruct((8,), F32)),
        in_specs=[hbm] * 7,
        out_specs=(hbm, hbm, scalar),
        scratch_shapes=[
            pltpu.SMEM((4, 8, 8), jnp.int32),
            pltpu.SMEM((4,), jnp.int32),
            pltpu.SMEM((4,), F32),
            pltpu.SMEM((14,), F32),
            pltpu.SMEM((64,), F32),
            flat,
            pltpu.VMEM((4, ROWS, ROWS), BF16),
            pltpu.VMEM((4, ROWS, ROWS), BF16),
            flat,
            cube,
            flat,
            flat,
            cube,
            cube,
            cube,
            wide,
            wide,
            pltpu.VMEM((LANES, ROWS), BF16),
            wide,
            wide,
            pltpu.VMEM((8, ROWS), F32),
            pltpu.VMEM((3, 2, 16, 8, LANES), F32),
            pltpu.VMEM((4, 16, 1, LANES), F32),
            pltpu.VMEM((4, 16, 1, LANES), F32),
            pltpu.VMEM((256, 1, LANES), F32),
            pltpu.VMEM((4, 1, LANES), F32),
            pltpu.VMEM((4, 1, LANES), F32),
            dma((7,)),
            dma((3,)),
            dma((2,)),
            dma((2,)),
            dma,
            dma((3,)),
            dma((3,)),
            dma((3, 2)),
            dma((3, 2)),
            dma((4,)),
            dma((4,)),
            dma((4,)),
            dma((4,)),
        ],
        compiler_params=pltpu.CompilerParams(
            collective_id=0, has_side_effects=True, vmem_limit_bytes=67043328
        ),
    )(state, operators, op_mask, site_bits, field, site_coupling, mode_coupling)
    return pl.pallas_call(
        finish_kernel,
        out_shape=(block, block, jax.ShapeDtypeStruct((STEPS,), F32)),
        in_specs=[hbm] * 3,
        out_specs=(hbm, hbm, hbm),
        scratch_shapes=[flat] * 3
        + [pltpu.SMEM((8,), F32), pltpu.SMEM((STEPS,), F32), dma((5,)), dma((8,))],
        compiler_params=pltpu.CompilerParams(vmem_limit_bytes=67043328),
    )(*carried)


def solution(mesh):
    in_specs = (P("site", "phonon"), P(), P(), P(), P(), P(), P())
    out_specs = (P("site", "phonon"), P("site", "phonon"), P())
    return jax.shard_map(shards, mesh=mesh, in_specs=in_specs, out_specs=out_specs, check_vma=False)
```

```python
import functools
import jax
import jax.numpy as jnp
from jax import lax
from jax.experimental import pallas as pl
from jax.experimental.pallas import tpu as pltpu
from jax.sharding import PartitionSpec as P

MESH = pl.DeviceIdType.MESH
F32 = jnp.float32
BF16 = jnp.bfloat16
ROWS = 1024
LANES = 128
STEPS = 3
EPSILON = 1e-06
ENTRIES = 33554432.0


def flipped(value, bit):
    size = 8 << bit
    parts = [value[i * size : (i + 1) * size] for i in range(LANES // size)]
    swapped = []
    for i in range(0, len(parts), 2):
        swapped += [parts[i + 1], parts[i]]
    return jnp.concatenate(swapped, axis=0)


def ring(offset, size):
    return min(offset % size, -offset % size)


def offsets(zs=1, xs=1, ys=1, cores=1):
    found = [
        (dz, dx, dy, dc)
        for dz in range(zs)
        for dx in range(xs)
        for dy in range(ys)
        for dc in range(cores)
        if (dz, dx, dy, dc) != (0, 0, 0, 0)
    ]
    return sorted(found, key=lambda o: -ring(o[0], 8) - ring(o[1], 4) - ring(o[2], 4))


PLANE = offsets(zs=8, xs=4, cores=2)
LINE = offsets(ys=4)
COLUMN = offsets(zs=8, cores=2)
LAYER = offsets(xs=4, ys=4)
ROW = offsets(xs=4)
WHOLE = offsets(zs=8, xs=4, ys=4, cores=2)


def finished(r, high):
    lower = r[pl.ds(high, 64, stride=16), :]
    upper = r[pl.ds(8 + high, 64, stride=16), :]
    return jnp.concatenate([lower, upper], axis=0).T


def kernel(
    state, ops, mask_in, site_bits_in, field_in, site_coupling_in, mode_coupling_in,
    r_3, ready, stats,
    mask, site_bits, field, site_coupling, mode_coupling,
    st, opv, a, t, r_in, r_2, out_2, w_1, w_2, w_3, u_0, u_1, ub, acc, linear, occ, halo,
    slots_1, slots_2, slots_whole, rows_1, rows_2,
    load_sem, self_sem, in_sem, line_sem, out_sem, send_sem, recv_sem, hsend_sem, hrecv_sem,
    send_1, recv_1, send_2, recv_2,
):
    site = lax.axis_index("site")
    phonon = lax.axis_index("phonon")
    z_lo, x = site // 4, site % 4
    y, q = phonon // 4, phonon % 4
    z_hi, core = q // 2, q % 2
    z = z_hi * 4 + z_lo
    mode = site * 4 + q

    def place_of(offset):
        dz, dx, dy, dc = offset
        z_at, x_at, y_at, core_at = (z + dz) % 8, (x + dx) % 4, (y + dy) % 4, (core + dc) % 2
        return (z_at % 4) * 4 + x_at, y_at, (z_at // 4) * 2 + core_at

    def device_of(offset):
        site_at, y_at, q_at = place_of(offset)
        return (site_at, y_at * 4 + q_at)

    barrier = pltpu.get_barrier_semaphore()
    for offset in PLANE + LINE:
        pl.semaphore_signal(barrier, inc=1, device_id=device_of(offset), device_id_type=MESH)

    load_state = pltpu.make_async_copy(state, st, load_sem.at[0])
    load_state.start()
    load_ops = pltpu.make_async_copy(ops, opv, load_sem.at[1])
    small = [
        pltpu.make_async_copy(source, target, load_sem.at[2 + i])
        for i, (source, target) in enumerate(
            (
                (mask_in, mask),
                (site_bits_in, site_bits),
                (field_in, field),
                (site_coupling_in, site_coupling),
                (mode_coupling_in, mode_coupling),
            )
        )
    ]
    for copy in small:
        copy.start()
    load_ops.start()

    load_state.wait()
    zero = jnp.zeros((8, LANES), F32)
    squares = zero
    for high in range(8):
        block = st[high * 128 : (high + 1) * 128, :]
        squares = squares + jnp.sum((block * block).reshape(16, 8, LANES), axis=0)
        turned = block.T
        t[pl.ds(high, 64, stride=16), :] = turned[:64]
        t[pl.ds(8 + high, 64, stride=16), :] = turned[64:]

    lane = lax.broadcasted_iota(jnp.int32, (1, LANES), 1)

    def fold(value):
        row = jnp.sum(value, axis=0, keepdims=True)
        return row + pltpu.roll(row, 64, 1)

    def wait_recv(ref, send, recv):
        pltpu.make_async_remote_copy(
            src_ref=ref, dst_ref=ref, send_sem=send, recv_sem=recv,
            device_id=(site, phonon), device_id_type=MESH,
        ).wait_recv()

    def wait_send(ref, send, recv):
        pltpu.make_async_remote_copy(
            src_ref=ref, dst_ref=ref, send_sem=send, recv_sem=recv,
            device_id=(site, phonon), device_id_type=MESH,
        ).wait_send()

    groups = {
        "line": (LINE, 4, y),
        "row": (ROW, 4, x),
        "column": (COLUMN, 16, z * 2 + core),
        "layer": (LAYER, 16, x * 4 + y),
        "whole": (WHOLE, 256, site * 16 + phonon),
    }

    def spread(group, src, slots, row, send, recv):
        members, count, index = groups[group]
        src[...] = row
        slots[index] = row
        for offset in members:
            pltpu.make_async_remote_copy(
                src_ref=src, dst_ref=slots.at[index], send_sem=send, recv_sem=recv,
                device_id=device_of(offset), device_id_type=MESH,
            ).start()

    def gather(group, slots, send, recv):
        members, count, index = groups[group]
        wait_recv(slots.at[pl.ds(0, count - 1)], send, recv)
        if count <= 16:
            return jnp.sum(slots[0:count], axis=0)
        value = slots[0:8]
        for i in range(8, count, 8):
            value = value + slots[i : i + 8]
        return jnp.sum(value, axis=0)

    def scalars_start(r, group, squares, products):
        row = jnp.where(lane < 64, fold(squares), fold(products))
        spread(group, rows_1.at[r], slots_1.at[r], row, send_1.at[r], recv_1.at[r])

    def scalars_middle(r, group, group_2):
        row = gather(group, slots_1.at[r], send_1.at[r], recv_1.at[r])
        spread(group_2, rows_2.at[r], slots_2.at[r], row, send_2.at[r], recv_2.at[r])

    def scalars_end(r, group_2):
        return measures(gather(group_2, slots_2.at[r], send_2.at[r], recv_2.at[r]))

    def measures(row):
        total = jnp.sum(jnp.where(lane < 64, row, 0.0), axis=1, keepdims=True)
        product = jnp.sum(jnp.where(lane < 64, 0.0, row), axis=1, keepdims=True)
        inverse = 1.0 / jnp.sqrt(total / ENTRIES + EPSILON)
        return inverse, product * inverse / ENTRIES

    def chunk2(ref, i):
        return ref.at[pl.ds(pl.multiple_of(i * 16, 16), 16), :]

    def chunk3(ref, site_at, q_at):
        return ref.at[site_at, pl.ds(pl.multiple_of(q_at * 16, 16), 16), :]

    early = (q == 0) | (q == 3)
    kind = jnp.where(early, 0, 1)

    def exchange_in_start():
        pltpu.make_async_copy(chunk2(t, mode), chunk3(r_in, site, q), in_sem.at[kind]).start()
        for offset in PLANE:
            site_at, y_at, q_at = place_of(offset)
            pltpu.make_async_remote_copy(
                src_ref=chunk2(t, site_at * 4 + q_at), dst_ref=chunk3(r_in, site, q),
                send_sem=send_sem.at[0], recv_sem=in_sem.at[kind],
                device_id=(site_at, y_at * 4 + q_at), device_id_type=MESH,
            ).start()

    def exchange_in_wait(which):
        wait_recv(t.at[pl.ds(0, 32 * 16), :], send_sem.at[0], in_sem.at[which])

    def exchange_out_self(e, w, r):
        return pltpu.make_async_copy(chunk3(w, site, q), chunk2(r, mode), self_sem.at[e])

    def exchange_out_start(e, w, r):
        exchange_out_self(e, w, r).start()
        for offset in PLANE:
            site_at, y_at, q_at = place_of(offset)
            pltpu.make_async_remote_copy(
                src_ref=chunk3(w, site_at, q_at), dst_ref=chunk2(r, mode),
                send_sem=send_sem.at[e], recv_sem=recv_sem.at[e],
                device_id=(site_at, y_at * 4 + q_at), device_id_type=MESH,
            ).start()

    def exchange_out_wait(e, w, r):
        exchange_out_self(e, w, r).wait()
        wait_recv(t.at[pl.ds(0, 63 * 16), :], send_sem.at[e], recv_sem.at[e])

    def halo_copies(k, w):
        up = pltpu.make_async_remote_copy(
            src_ref=w.at[:, pl.ds(56, 8), :], dst_ref=halo.at[k, 0],
            send_sem=hsend_sem.at[k, 0], recv_sem=hrecv_sem.at[k, 0],
            device_id=(site, ((y + 1) % 4) * 4 + q), device_id_type=MESH,
        )
        down = pltpu.make_async_remote_copy(
            src_ref=w.at[:, pl.ds(0, 8), :], dst_ref=halo.at[k, 1],
            send_sem=hsend_sem.at[k, 1], recv_sem=hrecv_sem.at[k, 1],
            device_id=(site, ((y + 3) % 4) * 4 + q), device_id_type=MESH,
        )
        return up, down

    pl.semaphore_wait(barrier, 66)
    scalars_start(0, "column", squares, zero)
    pl.when(early)(exchange_in_start)

    for copy in small:
        copy.wait()
    chosen = [site_bits[b] for b in range(4)]
    fields = [field[c] for c in chosen]
    device_coupling = [site_coupling[c] for c in chosen]

    place = lax.broadcasted_iota(jnp.int32, (8, ROWS), 1)
    weights = jnp.zeros((8, ROWS), F32)
    for j in range(10):
        weights = weights + site_coupling[4 + j] * ((place >> j) & 1).astype(F32)
    occ[...] = weights

    level = lax.broadcasted_iota(jnp.int32, (8, LANES), 0) + y * 8
    mode_weight = mode_coupling[mode] / jnp.sqrt(F32(32.0))
    lower_weight = mode_weight * jnp.sqrt(level.astype(F32))
    upper_weight = mode_weight * jnp.where(level < 31, jnp.sqrt((level + 1).astype(F32)), 0.0)

    load_ops.wait()

    def mask_operator(b):
        @pl.loop(0, 8)
        def _(i):
            rows = pl.ds(pl.multiple_of(i * 128, 128), 128)
            for j in range(8):
                keep = mask[chosen[b], i, j] > 0
                tile = opv[chosen[b], rows, j * 128 : (j + 1) * 128]
                a[b, j * 128 : (j + 1) * 128, rows] = jnp.where(keep, tile, jnp.zeros_like(tile)).T

    for b in range(4):
        mask_operator(b)
    pl.when(jnp.logical_not(early))(exchange_in_start)
    scalars_middle(0, "column", "row")
    row = gather("row", slots_2.at[0], send_2.at[0], recv_2.at[0])
    spread("line", rows_1.at[1], slots_1.at[1], row, line_sem.at[0], line_sem.at[1])
    exchange_in_wait(0)
    for copy in halo_copies(0, r_in):
        copy.start()
    exchange_in_wait(1)
    inverse, _ = measures(gather("line", slots_1.at[1], line_sem.at[0], line_sem.at[1]))

    sublane = lax.broadcasted_iota(jnp.int32, (8, LANES), 0)

    def normalize(w, u, inverse):
        scale = jnp.broadcast_to(inverse, (8, LANES))

        @pl.loop(0, 8)
        def _(e):
            for high in range(8):
                cols = slice(high * 128, (high + 1) * 128)
                first = w[2 * e, pl.ds(high, 8, stride=8), :] * scale
                second = w[2 * e + 1, pl.ds(high, 8, stride=8), :] * scale
                both = jnp.concatenate([first, second], axis=0)
                rows = pl.ds(pl.multiple_of(e * 16, 16), 16)
                if u is not None:
                    u[rows, cols] = both
                ub[rows, cols] = both.astype(BF16)

    def bits_of(d):
        if isinstance(d, int):
            return [jnp.int32((d >> b) & 1) for b in range(4)]
        return [(d // (1 << b)) % 2 for b in range(4)]

    def occupancy(d, high):
        constant = F32(0.0)
        for b, bit in enumerate(bits_of(d)):
            constant = constant + device_coupling[b] * bit.astype(F32)
        return occ[:, high * 128 : (high + 1) * 128] + constant

    def halo_rows(k, d, high):
        below = jnp.broadcast_to(halo[k, 0, d, high : high + 1, :], (8, LANES))
        above = jnp.broadcast_to(halo[k, 1, d, high : high + 1, :], (8, LANES))
        return below, above

    def ladder_of(k, d, high, here):
        below, above = halo_rows(k, d, high)
        lower = jnp.where(sublane == 0, below, pltpu.roll(here, 1, 0))
        upper = jnp.where(sublane == 7, above, pltpu.roll(here, 7, 0))
        return occupancy(d, high) * (lower_weight * lower + upper_weight * upper)

    def prepare(k, w_before, w):
        for copy in halo_copies(k, w):
            copy.wait_recv()

        @pl.loop(0, 16)
        def _(d):
            bits = bits_of(d)
            rows = pl.ds(pl.multiple_of(d * 8, 8), 8)
            for high in range(8):
                cols = slice(high * 128, (high + 1) * 128)
                here = w_before[d, pl.ds(high, 8, stride=8), :]
                value = ladder_of(k, d, high, here)
                for b in range(4):
                    other = d + (1 - 2 * bits[b]) * (1 << b)
                    value = value + fields[b] * w_before[other, pl.ds(high, 8, stride=8), :]
                linear[rows, cols] = value

    def first_step(w, inverse):
        scale = jnp.broadcast_to(inverse, (8, LANES))
        total = None
        for b in range(4):
            product = flipped(jnp.dot(ub[...], a[b], preferred_element_type=F32), b)
            total = product if total is None else total + product
        inner_lower = jnp.where(sublane == 0, 0.0, lower_weight)
        inner_upper = jnp.where(sublane == 7, 0.0, upper_weight)
        for d in range(16):
            rows = slice(d * 8, (d + 1) * 8)
            for high in range(8):
                cols = slice(high * 128, (high + 1) * 128)
                here = r_in[d, pl.ds(high, 8, stride=8), :]
                value = occupancy(d, high) * (
                    inner_lower * pltpu.roll(here, 1, 0) + inner_upper * pltpu.roll(here, 7, 0)
                )
                for b in range(4):
                    value = value + fields[b] * r_in[d ^ (1 << b), pl.ds(high, 8, stride=8), :]
                acc[rows, cols] = total[rows, cols] + value * scale
        for copy in halo_copies(0, r_in):
            copy.wait_recv()
        outer_lower = jnp.where(sublane == 0, lower_weight, 0.0) * scale
        outer_upper = jnp.where(sublane == 7, upper_weight, 0.0) * scale
        squares, products = zero, zero
        for d in range(16):
            rows = slice(d * 8, (d + 1) * 8)
            for high in range(8):
                cols = slice(high * 128, (high + 1) * 128)
                below, above = halo_rows(0, d, high)
                new = acc[rows, cols] + occupancy(d, high) * (
                    outer_lower * below + outer_upper * above
                )
                w[d, pl.ds(high, 8, stride=8), :] = new
                squares = squares + new * new
                products = products + u_0[rows, cols] * new
        return squares, products

    def step(u_before, w, inverse, part):
        scale = jnp.broadcast_to(inverse, (8, LANES))
        total = None
        for b in range(4):
            product = flipped(jnp.dot(ub[...], a[b], preferred_element_type=F32), b)
            total = product if total is None else total + product
        squares, products = zero, zero
        for d in range(16):
            rows = slice(d * 8, (d + 1) * 8)
            for high in range(8):
                cols = slice(high * 128, (high + 1) * 128)
                new = total[rows, cols] + part(d, high) * scale
                new = 2.0 * new - u_before[rows, cols] * scale
                w[d, pl.ds(high, 8, stride=8), :] = new
                squares = squares + new * new
                products = products + u_0[rows, cols] * new
        return squares, products

    def set_stat(k, value):
        stats[k] = value[0, 0]

    normalize(r_in, u_0, inverse)
    squares, products = first_step(w_1, inverse)
    row = jnp.where(lane < 64, fold(squares), fold(products))
    spread("whole", rows_2.at[1], slots_whole, row, send_1.at[1], recv_1.at[1])
    for copy in halo_copies(1, w_1):
        copy.start()
    prepare(1, w_1, w_2)
    inverse, moment = measures(gather("whole", slots_whole, send_1.at[1], recv_1.at[1]))
    set_stat(0, moment)

    normalize(w_1, u_1, inverse)
    squares, products = step(
        u_0, w_2, inverse,
        lambda d, high: linear[d * 8 : (d + 1) * 8, high * 128 : (high + 1) * 128],
    )
    scalars_start(2, "column", squares, products)
    for copy in halo_copies(2, w_2):
        copy.start()
    exchange_out_start(1, w_2, r_2)
    prepare(2, w_2, w_3)
    scalars_middle(2, "column", "layer")
    inverse, moment = scalars_end(2, "layer")
    set_stat(1, moment)
    inverse_2 = inverse

    normalize(w_2, None, inverse)
    squares, products = step(
        u_1, w_3, inverse,
        lambda d, high: linear[d * 8 : (d + 1) * 8, high * 128 : (high + 1) * 128],
    )
    scalars_start(3, "column", squares, products)
    exchange_out_start(2, w_3, r_3)
    scalars_middle(3, "column", "layer")
    exchange_out_wait(1, w_2, r_2)
    scale_2 = jnp.broadcast_to(inverse_2, (128, LANES))
    for high in range(8):
        out_2[high * 128 : (high + 1) * 128, :] = finished(r_2, high) * scale_2
    store_2 = pltpu.make_async_copy(out_2, ready, out_sem)
    store_2.start()
    inverse, moment = scalars_end(3, "layer")
    set_stat(2, moment)
    set_stat(3, inverse)
    exchange_out_wait(2, w_3, r_3)
    store_2.wait()

    for e in range(3):
        wait_send(t.at[pl.ds(0, 63 * 16), :], send_sem.at[e], recv_sem.at[e])
    wait_send(slots_1.at[1, pl.ds(0, 3)], line_sem.at[0], line_sem.at[1])
    wait_send(slots_whole.at[pl.ds(0, 255)], send_1.at[1], recv_1.at[1])
    for r, group, group_2 in (
        (0, "column", "row"),
        (2, "column", "layer"),
        (3, "column", "layer"),
    ):
        count, count_2 = groups[group][1], groups[group_2][1]
        wait_send(slots_1.at[r, pl.ds(0, count - 1)], send_1.at[r], recv_1.at[r])
        wait_send(slots_2.at[r, pl.ds(0, count_2 - 1)], send_2.at[r], recv_2.at[r])
    for k, w in enumerate((r_in, w_1, w_2)):
        for copy in halo_copies(k, w):
            copy.wait_send()


def finish_kernel(r_3, ready, stats, last, prev, moments, v_3, v_2, out_3, held, kept, sem, store_sem):
    load = pltpu.make_async_copy(stats, held, sem.at[0])
    load_3 = pltpu.make_async_copy(r_3, v_3, sem.at[1])
    load_2 = pltpu.make_async_copy(ready, v_2, sem.at[2])
    store = pltpu.make_async_copy(kept, moments, sem.at[3])
    store_2 = pltpu.make_async_copy(v_2, prev, sem.at[4])
    load_3.start()
    load.start()
    load_2.start()
    load.wait()
    for k in range(STEPS):
        kept[k] = held[k]
    store.start()
    load_3.wait()
    scale = held[3]
    stores = []
    for high in range(8):
        rows = pl.ds(high * 128, 128)
        out_3[rows, :] = finished(v_3, high) * scale
        stores.append(pltpu.make_async_copy(out_3.at[rows, :], last.at[rows, :], store_sem.at[high]))
        stores[high].start()
    load_2.wait()
    store_2.start()
    for copy in stores + [store, store_2]:
        copy.wait()


def shards(state, operators, op_mask, site_bits, field, site_coupling, mode_coupling):
    block = jax.ShapeDtypeStruct((ROWS, LANES), F32)
    flat = pltpu.VMEM((ROWS, LANES), F32)
    cube = pltpu.VMEM((16, 64, LANES), F32)
    wide = pltpu.VMEM((LANES, ROWS), F32)
    dma = pltpu.SemaphoreType.DMA
    hbm = pl.BlockSpec(memory_space=pltpu.HBM)
    scalar = pl.BlockSpec(memory_space=pltpu.SMEM)
    carried = pl.pallas_call(
        kernel,
        out_shape=(block, block, jax.ShapeDtypeStruct((8,), F32)),
        in_specs=[hbm] * 7,
        out_specs=(hbm, hbm, scalar),
        scratch_shapes=[
            pltpu.SMEM((4, 8, 8), jnp.int32),
            pltpu.SMEM((4,), jnp.int32),
            pltpu.SMEM((4,), F32),
            pltpu.SMEM((14,), F32),
            pltpu.SMEM((64,), F32),
            flat,
            pltpu.VMEM((4, ROWS, ROWS), BF16),
            pltpu.VMEM((4, ROWS, ROWS), BF16),
            flat,
            cube,
            flat,
            flat,
            cube,
            cube,
            cube,
            wide,
            wide,
            pltpu.VMEM((LANES, ROWS), BF16),
            wide,
            wide,
            pltpu.VMEM((8, ROWS), F32),
            pltpu.VMEM((3, 2, 16, 8, LANES), F32),
            pltpu.VMEM((4, 16, 1, LANES), F32),
            pltpu.VMEM((4, 16, 1, LANES), F32),
            pltpu.VMEM((256, 1, LANES), F32),
            pltpu.VMEM((4, 1, LANES), F32),
            pltpu.VMEM((4, 1, LANES), F32),
            dma((7,)),
            dma((3,)),
            dma((2,)),
            dma((2,)),
            dma,
            dma((3,)),
            dma((3,)),
            dma((3, 2)),
            dma((3, 2)),
            dma((4,)),
            dma((4,)),
            dma((4,)),
            dma((4,)),
        ],
        compiler_params=pltpu.CompilerParams(
            collective_id=0, has_side_effects=True, vmem_limit_bytes=67043328
        ),
    )(state, operators, op_mask, site_bits, field, site_coupling, mode_coupling)
    return pl.pallas_call(
        finish_kernel,
        out_shape=(block, block, jax.ShapeDtypeStruct((STEPS,), F32)),
        in_specs=[hbm] * 3,
        out_specs=(hbm, hbm, hbm),
        scratch_shapes=[flat] * 3
        + [pltpu.SMEM((8,), F32), pltpu.SMEM((STEPS,), F32), dma((5,)), dma((8,))],
        compiler_params=pltpu.CompilerParams(vmem_limit_bytes=67043328),
    )(*carried)


def solution(mesh):
    in_specs = (P("site", "phonon"), P(), P(), P(), P(), P(), P())
    out_specs = (P("site", "phonon"), P("site", "phonon"), P())
    return jax.shard_map(shards, mesh=mesh, in_specs=in_specs, out_specs=out_specs, check_vma=False)
```
